256 devices in a mesh: group: 8 (over y, core), tile: 32 (over z, x).
Axes of the slice: x: 4, y: 4, z: 8, core: 2. Of those that a mesh axis runs over, the one named last changes fastest.
Arguments:
- radiance: bfloat16 [224, 3072, 1024], P(None, 'tile', 'group'), may hold values from -200 to 200
- valid_mask: int32 [3072, 1024], P('tile', 'group'), may hold values 0 or 1
Outputs:
- whitened: bfloat16 [224, 3072, 1024], P(None, 'tile', 'group')
- whitened_cov: float32 [224, 224], replicated
The draws below stay inside these ranges and needn't reach their ends.
All inputs are finite; a program needn't handle non-finite values. No bound on the sum of `valid_mask` on one device may be relied on, other than what follows from the above.
Results may differ from the reference program's by a relative error of at most 0.0058.
Values may be sent and summed in bfloat16 or wider, within the bound.
No kernel may reach another device: no remote copies, remote signals or barrier semaphores. Data moves between devices by JAX's collectives and lax.ppermute only.
A program may use at most 128 MiB of HBM per device.

```python
import math
import jax
import jax.numpy as jnp
from jax import lax

B = 224
ROW_DEV = 96
COL_DEV = 128
ROWS = 3072
COLS = 1024
N_GROUP = 8


def draw_radiance(key, part):
    keys = jax.random.split(jax.random.fold_in(key, 11), 12)
    shape = (B, ROWS, COLS)
    fine = jnp.clip(jax.random.normal(keys[0], shape, jnp.float32), -5.0, 5.0)
    common = jnp.clip(jax.random.normal(keys[1], (ROWS, COLS), jnp.float32), -5.0, 5.0)
    raw_patch = jnp.clip(jax.random.normal(keys[10], shape, jnp.float32), -5.0, 5.0)
    row_pos = jnp.arange(ROWS, dtype=jnp.float32)[:, None]
    col_pos = jnp.arange(COLS, dtype=jnp.float32)[None, :]
    freq = jax.random.uniform(keys[2], (4,), jnp.float32, 0.02, 0.08)
    phase = jax.random.uniform(keys[3], (4,), jnp.float32, 0.0, 6.283)
    wave_one = jnp.sin(freq[0] * row_pos + phase[0]) * jnp.cos(freq[1] * col_pos + phase[1])
    wave_two = jnp.cos(freq[2] * row_pos + phase[2]) * jnp.sin(freq[3] * col_pos + phase[3])
    loading_a = jnp.clip(jax.random.normal(keys[4], (B, 1, 1), jnp.float32), -2.0, 2.0)
    loading_g = jnp.clip(jax.random.normal(keys[5], (B, 1, 1), jnp.float32), -2.0, 2.0)
    loading_h = jnp.clip(jax.random.normal(keys[6], (B, 1, 1), jnp.float32), -2.0, 2.0)
    band_scale = jnp.exp(jax.random.uniform(keys[7], (B, 1, 1), jnp.float32, math.log(0.5), math.log(2.0)))
    pixel_scale = jnp.exp(jax.random.uniform(keys[8], (1, ROWS, COLS), jnp.float32, 0.0, math.log(10.0)))
    tile_of_row = jnp.arange(ROWS, dtype=jnp.int32)[:, None] // ROW_DEV
    group_of_col = jnp.arange(COLS, dtype=jnp.int32)[None, :] // COL_DEV
    block_index = group_of_col * (ROWS // ROW_DEV) + tile_of_row
    chosen = jax.random.randint(keys[9], (2,), 0, ROWS // ROW_DEV * (COLS // COL_DEV))
    heavy = jnp.logical_or(block_index == chosen[0], block_index == chosen[1])
    wave_gain = jnp.where(heavy, 8.0, 1.0).astype(jnp.float32)[None]
    padded_raw = jnp.pad(raw_patch, ((0, 0), (4, 4), (4, 4)))
    row_box = padded_raw[:, 0:ROWS]
    for offset in range(1, 9):
        row_box = row_box + padded_raw[:, offset:offset + ROWS]
    col_box = row_box[:, :, 0:COLS]
    for offset in range(1, 9):
        col_box = col_box + row_box[:, :, offset:offset + COLS]
    patches = col_box / 9.0
    far_shift = jax.random.randint(keys[11], (), 2, B - 1)
    mixture = patches + 0.8 * jnp.roll(patches, 1, axis=0) + 0.5 * jnp.roll(patches, far_shift, axis=0)
    field = band_scale * (0.3 * pixel_scale * (fine + loading_h * common[None]) + 1.5 * wave_gain * (loading_a * wave_one[None] + loading_g * wave_two[None]) + mixture)
    field = jnp.clip(field, -200.0, 200.0)
    return field.astype(jnp.bfloat16)


def touch_ends(drawn, own_key, smallest, high):
    place = [jax.random.randint(jax.random.fold_in(own_key, axis), (), 0, length) for axis, length in enumerate(drawn.shape)]
    main_axis = drawn.shape.index(max(drawn.shape))
    next_to = place[:main_axis] + [(place[main_axis] + 1) % drawn.shape[main_axis]] + place[main_axis + 1:]
    return drawn.at[tuple(place)].set(smallest).at[tuple(next_to)].set(high)


def setup_inputs(seed: int = 0) -> dict:
    key_of = jax.random.split(jax.random.key(seed), 3)
    return {
        "radiance": draw_radiance(jax.random.fold_in(key_of[2], 71), 0),
        "valid_mask": touch_ends((jax.random.randint(key_of[1], (ROWS, COLS), 0, 8) < 7).astype(jnp.int32), jax.random.fold_in(key_of[1], 1), 0, 1),
    }


def smooth_noise(padded, rows, cols):
    field = padded.astype(jnp.float32)
    row_smooth = (field[:, 0:rows] + 4.0 * field[:, 1:rows + 1] + 6.0 * field[:, 2:rows + 2] + 4.0 * field[:, 3:rows + 3] + field[:, 4:rows + 4]) / 16.0
    smooth = (row_smooth[:, :, 0:cols] + 4.0 * row_smooth[:, :, 1:cols + 1] + 6.0 * row_smooth[:, :, 2:cols + 2] + 4.0 * row_smooth[:, :, 3:cols + 3] + row_smooth[:, :, 4:cols + 4]) / 16.0
    centre = field[:, 2:rows + 2, 2:cols + 2]
    noise = centre - 0.5 * (field[:, 1:rows + 1, 2:cols + 2] + field[:, 3:rows + 3, 2:cols + 2])
    return (smooth, noise)

def finish(signal_moment, noise_moment, signal_first, noise_first, count):
    signal_cov = (signal_moment - jnp.outer(signal_first, signal_first) / count) / (count - 1.0)
    noise_cov = (noise_moment - jnp.outer(noise_first, noise_first) / count) / (count - 1.0)
    lower = jnp.linalg.cholesky(noise_cov)
    identity = jnp.eye(signal_first.shape[0], dtype=jnp.float32)
    inverse_lower = jax.scipy.linalg.solve_triangular(lower, identity, lower=True)
    left = jnp.dot(inverse_lower, signal_cov, precision=lax.Precision.HIGHEST)
    whitened_cov = jnp.dot(left, inverse_lower.T, precision=lax.Precision.HIGHEST)
    return (inverse_lower, whitened_cov)

def reference(radiance, valid_mask):
    padded_all = jnp.pad(radiance, ((0, 0), (2, 2), (2, 2)))
    starts = jnp.arange(N_GROUP, dtype=jnp.int32)

    def strip_fields(index):
        start = (index * COL_DEV).astype(jnp.int32)
        strip = lax.dynamic_slice_in_dim(padded_all, start, COL_DEV + 4, 2)
        smooth, noise = smooth_noise(strip, ROWS, COL_DEV)
        weight = lax.dynamic_slice_in_dim(valid_mask, start, COL_DEV, 1).astype(jnp.float32)[None]
        return (smooth, noise, weight)

    def accumulate(carry, index):
        smooth, noise, weight = strip_fields(index)
        signal_masked = smooth * weight
        noise_masked = noise * weight
        signal_flat = signal_masked.astype(jnp.bfloat16).reshape(B, ROWS * COL_DEV)
        noise_flat = noise_masked.astype(jnp.bfloat16).reshape(B, ROWS * COL_DEV)
        dims = (((1,), (1,)), ((), ()))
        signal_moment = lax.dot_general(signal_flat.astype(jnp.float32), signal_flat.astype(jnp.float32), dims, preferred_element_type=jnp.float32)
        noise_moment = lax.dot_general(noise_flat.astype(jnp.float32), noise_flat.astype(jnp.float32), dims, preferred_element_type=jnp.float32)
        terms = (signal_moment, noise_moment, jnp.sum(signal_masked, axis=(1, 2)), jnp.sum(noise_masked, axis=(1, 2)), jnp.sum(weight))
        return (tuple((a + b for a, b in zip(carry, terms))), None)
    start_state = (jnp.zeros((B, B), jnp.float32), jnp.zeros((B, B), jnp.float32), jnp.zeros((B,), jnp.float32), jnp.zeros((B,), jnp.float32), jnp.zeros((), jnp.float32))
    totals, _ = lax.scan(accumulate, start_state, starts)
    signal_moment, noise_moment, signal_first, noise_first, count = totals
    inverse_lower, whitened_cov = finish(signal_moment, noise_moment, signal_first, noise_first, count)
    inverse_cast = inverse_lower.astype(jnp.bfloat16)
    mean_signal = signal_first / count

    def whiten(index):
        smooth, _, weight = strip_fields(index)
        centered = (weight * (smooth - mean_signal[:, None, None])).astype(jnp.bfloat16).reshape(B, ROWS * COL_DEV)
        product = jnp.dot(inverse_cast.astype(jnp.float32), centered.astype(jnp.float32), preferred_element_type=jnp.float32)
        return product.astype(jnp.bfloat16).reshape(B, ROWS, COL_DEV)
    pieces = lax.map(whiten, starts)
    whitened = jnp.transpose(pieces, (1, 2, 0, 3)).reshape(B, ROWS, COLS)
    return (whitened, whitened_cov)
```

```python
import jax
import jax.numpy as jnp
from jax import lax
from jax.sharding import PartitionSpec as P


def padded_2(block, sides, width):
    for axis, dim in sides:
        count = lax.axis_size(axis)
        forward = [(i, i + 1) for i in range(count - 1)]
        backward = [(target, source) for source, target in forward]
        low = lax.ppermute(
            lax.slice_in_dim(block, block.shape[dim] - width, None, axis=dim), axis, forward
        )
        high = lax.ppermute(lax.slice_in_dim(block, 0, width, axis=dim), axis, backward)
        block = jnp.concatenate([low, block, high], axis=dim)
    return block


def smooth_noise(padded, rows, cols):
    field = padded.astype(jnp.float32)
    row_smooth = (
        field[:, 0:rows]
        + 4.0 * field[:, 1 : rows + 1]
        + 6.0 * field[:, 2 : rows + 2]
        + 4.0 * field[:, 3 : rows + 3]
        + field[:, 4 : rows + 4]
    ) / 16.0
    smooth = (
        row_smooth[:, :, 0:cols]
        + 4.0 * row_smooth[:, :, 1 : cols + 1]
        + 6.0 * row_smooth[:, :, 2 : cols + 2]
        + 4.0 * row_smooth[:, :, 3 : cols + 3]
        + row_smooth[:, :, 4 : cols + 4]
    ) / 16.0
    centre = field[:, 2 : rows + 2, 2 : cols + 2]
    noise = centre - 0.5 * (
        field[:, 1 : rows + 1, 2 : cols + 2] + field[:, 3 : rows + 3, 2 : cols + 2]
    )
    return (smooth, noise)


def flat_pairs(sizes, move):
    y_size, z_size, x_size = sizes
    pairs = []
    for y in range(y_size):
        for core in range(2):
            for z in range(z_size):
                for x in range(x_size):
                    y2, core2, z2, x2 = move(y, core, z, x)
                    source = ((y * 2 + core) * z_size + z) * x_size + x
                    target = ((y2 * 2 + core2) * z_size + z2) * x_size + x2
                    pairs.append((source, target))
    return pairs


SIZES = (4, 8, 4)
STAGES = (
    [flat_pairs(SIZES, lambda y, c, z, x: (y, 1 - c, z, x))],
    [flat_pairs(SIZES, lambda y, c, z, x, k=k: (y, c, z, x ^ k)) for k in (1, 2, 3)],
    [flat_pairs(SIZES, lambda y, c, z, x, k=k: (y ^ k, c, z, x)) for k in (1, 2, 3)],
    [flat_pairs(SIZES, lambda y, c, z, x, k=k: (y, c, z ^ k, x)) for k in (1, 2, 3)],
    [flat_pairs(SIZES, lambda y, c, z, x: (y, c, 7 - z, x))],
)


def total_of(value):
    for stage in STAGES:
        parts = [lax.ppermute(value, ("group", "tile"), pairs) for pairs in stage]
        if len(parts) == 1:
            value = value + parts[0]
        else:
            value = (value + parts[0]) + (parts[1] + parts[2])
    return value


def finish(signal_moment, noise_moment, signal_first, noise_first, count):
    signal_cov = (signal_moment - jnp.outer(signal_first, signal_first) / count) / (count - 1.0)
    noise_cov = (noise_moment - jnp.outer(noise_first, noise_first) / count) / (count - 1.0)
    lower = jnp.linalg.cholesky(noise_cov)
    identity = jnp.eye(signal_first.shape[0], dtype=jnp.float32)
    inverse_lower = jax.scipy.linalg.solve_triangular(lower, identity, lower=True)
    left = jnp.dot(inverse_lower, signal_cov, precision=lax.Precision.HIGHEST)
    whitened_cov = jnp.dot(left, inverse_lower.T, precision=lax.Precision.HIGHEST)
    return (inverse_lower, whitened_cov)


def body(radiance, valid_mask):
    bands, rows, cols = radiance.shape
    padded = padded_2(radiance, (("group", 2), ("tile", 1)), 2)
    smooth, noise = smooth_noise(padded, rows, cols)
    weight = valid_mask.astype(jnp.float32)[None]
    signal_masked = smooth * weight
    noise_masked = noise * weight
    signal_first = jnp.sum(signal_masked, axis=(1, 2))
    noise_first = jnp.sum(noise_masked, axis=(1, 2))
    count = jnp.sum(weight)
    signal_flat = signal_masked.astype(jnp.bfloat16).reshape(bands, rows * cols)
    noise_flat = noise_masked.astype(jnp.bfloat16).reshape(bands, rows * cols)
    dims = (((1,), (1,)), ((), ()))
    signal_moment = lax.dot_general(
        signal_flat, signal_flat, dims, preferred_element_type=jnp.float32
    )
    noise_moment = lax.dot_general(noise_flat, noise_flat, dims, preferred_element_type=jnp.float32)
    count_column = jnp.full((bands,), count, jnp.float32)
    side = jnp.stack([signal_first, noise_first, count_column], axis=1)
    total = total_of(jnp.concatenate([signal_moment, noise_moment, side], axis=1))
    signal_total = total[:, :bands]
    noise_total = total[:, bands : 2 * bands]
    total_side = total[:, 2 * bands :]
    count_total = total_side[0, 2]
    signal_sum = total_side[:, 0]
    inverse_lower, whitened_cov = finish(
        signal_total, noise_total, signal_sum, total_side[:, 1], count_total
    )
    inverse_cast = inverse_lower.astype(jnp.bfloat16)
    mean_signal = signal_sum / count_total
    centered = (
        (weight * (smooth - mean_signal[:, None, None]))
        .astype(jnp.bfloat16)
        .reshape(bands, rows * cols)
    )
    product = jnp.dot(inverse_cast, centered, preferred_element_type=jnp.float32)
    whitened = product.astype(jnp.bfloat16).reshape(bands, rows, cols)
    return (whitened, whitened_cov)


def solution(mesh):
    return jax.shard_map(
        body,
        mesh=mesh,
        in_specs=(P(None, "tile", "group"), P("tile", "group")),
        out_specs=(P(None, "tile", "group"), P()),
        check_vma=False,
    )
```

```python
import jax
import jax.numpy as jnp
from jax import lax
from jax.experimental import pallas as pl
from jax.experimental.pallas import tpu as pltpu
from jax.sharding import PartitionSpec as P


def padded_2(block, sides, width):
    for axis, dim in sides:
        count = lax.axis_size(axis)
        forward = [(i, i + 1) for i in range(count - 1)]
        backward = [(target, source) for source, target in forward]
        low = lax.ppermute(
            lax.slice_in_dim(block, block.shape[dim] - width, None, axis=dim), axis, forward
        )
        high = lax.ppermute(lax.slice_in_dim(block, 0, width, axis=dim), axis, backward)
        block = jnp.concatenate([low, block, high], axis=dim)
    return block


def smooth_noise(padded, rows, cols):
    field = padded.astype(jnp.float32)
    row_smooth = (
        field[:, 0:rows]
        + 4.0 * field[:, 1 : rows + 1]
        + 6.0 * field[:, 2 : rows + 2]
        + 4.0 * field[:, 3 : rows + 3]
        + field[:, 4 : rows + 4]
    ) / 16.0
    smooth = (
        row_smooth[:, :, 0:cols]
        + 4.0 * row_smooth[:, :, 1 : cols + 1]
        + 6.0 * row_smooth[:, :, 2 : cols + 2]
        + 4.0 * row_smooth[:, :, 3 : cols + 3]
        + row_smooth[:, :, 4 : cols + 4]
    ) / 16.0
    centre = field[:, 2 : rows + 2, 2 : cols + 2]
    noise = centre - 0.5 * (
        field[:, 1 : rows + 1, 2 : cols + 2] + field[:, 3 : rows + 3, 2 : cols + 2]
    )
    return (smooth, noise)


def flat_pairs(sizes, move):
    y_size, z_size, x_size = sizes
    pairs = []
    for y in range(y_size):
        for core in range(2):
            for z in range(z_size):
                for x in range(x_size):
                    y2, core2, z2, x2 = move(y, core, z, x)
                    source = ((y * 2 + core) * z_size + z) * x_size + x
                    target = ((y2 * 2 + core2) * z_size + z2) * x_size + x2
                    pairs.append((source, target))
    return pairs


SIZES = (4, 8, 4)
CORE_SWAP = flat_pairs(SIZES, lambda y, c, z, x: (y, 1 - c, z, x))
STAGES = (
    [flat_pairs(SIZES, lambda y, c, z, x, k=k: (y, c, z, x ^ k)) for k in (1, 2, 3)],
    [flat_pairs(SIZES, lambda y, c, z, x, k=k: (y ^ k, c, z, x)) for k in (1, 2, 3)],
    [flat_pairs(SIZES, lambda y, c, z, x, k=k: (y, c, z ^ k, x)) for k in (1, 2, 3)],
    [flat_pairs(SIZES, lambda y, c, z, x: (y, c, 7 - z, x))],
)
AXES = ("group", "tile")


def total_of(value):
    half = value.shape[0] // 2
    core = lax.axis_index("group") % 2
    own = lax.dynamic_slice_in_dim(value, core * half, half, axis=0)
    other = lax.dynamic_slice_in_dim(value, (1 - core) * half, half, axis=0)
    own = own + lax.ppermute(other, AXES, CORE_SWAP)
    for stage in STAGES:
        parts = [lax.ppermute(own, AXES, pairs) for pairs in stage]
        if len(parts) == 1:
            own = own + parts[0]
        else:
            own = (own + parts[0]) + (parts[1] + parts[2])
    other = lax.ppermute(own, AXES, CORE_SWAP)
    first = core == 0
    return jnp.concatenate(
        [jnp.where(first, own, other), jnp.where(first, other, own)], axis=0
    )


def split_three(value):
    first = value.astype(jnp.bfloat16)
    rest = value - first.astype(jnp.float32)
    second = rest.astype(jnp.bfloat16)
    third = (rest - second.astype(jnp.float32)).astype(jnp.bfloat16)
    return (first, second, third)


def inverse_factor_kernel(cov_ref, out_ref, work_ref):
    size = cov_ref.shape[0]
    width = work_ref.shape[1]
    sub = lax.broadcasted_iota(jnp.int32, (8, 128), 0)
    lane = lax.broadcasted_iota(jnp.int32, (8, width), 1)
    sub_wide = lax.broadcasted_iota(jnp.int32, (8, width), 0)
    work_ref[...] = jnp.zeros_like(work_ref)
    work_ref[:, :size] = cov_ref[...]
    for block in range(size // 8):
        base, low = 8 * block, 8 * block + 8
        panel = work_ref[base:low, :]
        cols = [
            jnp.broadcast_to(panel[:, base + j : base + j + 1], (8, 128)) for j in range(8)
        ]
        eye = jnp.where(lane - base == sub_wide, 1.0, 0.0)
        rows = jnp.where((lane >= base) & (lane < low), eye, panel)
        scale = jnp.zeros((8, 128), jnp.float32)
        for j in range(8):
            root = lax.rsqrt(jnp.broadcast_to(cols[j][j : j + 1, :], (8, 128)))
            scale = jnp.where(sub == j, root, scale)
            if j < 7:
                ratio = jnp.where(sub > j, cols[j] * (root * root), 0.0)
                for i in range(j + 1, 8):
                    cols[i] = cols[i] - ratio * jnp.broadcast_to(cols[i][j : j + 1, :], (8, 128))
                ratio_wide = jnp.concatenate([ratio, ratio], axis=1)
                rows = rows - ratio_wide * jnp.broadcast_to(rows[j : j + 1, :], (8, width))
        rows = rows * jnp.concatenate([scale, scale], axis=1)
        work_ref[base:low, :] = jnp.where(lane < low, rows, 0.0)
        if low < size:
            one, two, three = split_three(rows)
            left = jnp.concatenate([one, one, two, two, one, three], axis=0)
            right = jnp.concatenate([one, two, one, two, three, one], axis=0)
            update = lax.dot_general(
                left, right, (((0,), (0,)), ((), ())), preferred_element_type=jnp.float32
            )
            rest = work_ref[low:size, :]
            rest_lane = lax.broadcasted_iota(jnp.int32, rest.shape, 1)
            rest = jnp.where((rest_lane >= base) & (rest_lane < low), 0.0, rest)
            work_ref[low:size, :] = rest - update[low:size, :]
    out_ref[...] = work_ref[:, :size]


def inverse_factor(cov):
    size = cov.shape[0]
    return pl.pallas_call(
        inverse_factor_kernel,
        out_shape=jax.ShapeDtypeStruct((size, size), jnp.float32),
        in_specs=[pl.BlockSpec(memory_space=pltpu.VMEM)],
        out_specs=pl.BlockSpec(memory_space=pltpu.VMEM),
        scratch_shapes=[pltpu.VMEM((size, 256), jnp.float32)],
        cost_estimate=pl.CostEstimate(
            flops=2 * size**3, bytes_accessed=8 * size**2, transcendentals=size
        ),
        name="inverse_factor",
    )(cov)


def finish(signal_moment, noise_moment, signal_first, noise_first, count):
    signal_cov = (signal_moment - jnp.outer(signal_first, signal_first) / count) / (count - 1.0)
    noise_cov = (noise_moment - jnp.outer(noise_first, noise_first) / count) / (count - 1.0)
    inverse_lower = inverse_factor(noise_cov)
    left = jnp.dot(inverse_lower, signal_cov, precision=lax.Precision.HIGHEST)
    whitened_cov = jnp.dot(left, inverse_lower.T, precision=lax.Precision.HIGHEST)
    return (inverse_lower, whitened_cov)


def body(radiance, valid_mask):
    bands, rows, cols = radiance.shape
    padded = padded_2(radiance, (("group", 2), ("tile", 1)), 2)
    smooth, noise = smooth_noise(padded, rows, cols)
    weight = valid_mask.astype(jnp.float32)[None]
    signal_masked = smooth * weight
    noise_masked = noise * weight
    signal_first = jnp.sum(signal_masked, axis=(1, 2))
    noise_first = jnp.sum(noise_masked, axis=(1, 2))
    count = jnp.sum(weight)
    signal_flat = signal_masked.astype(jnp.bfloat16).reshape(bands, rows * cols)
    noise_flat = noise_masked.astype(jnp.bfloat16).reshape(bands, rows * cols)
    dims = (((1,), (1,)), ((), ()))
    signal_moment = lax.dot_general(
        signal_flat, signal_flat, dims, preferred_element_type=jnp.float32
    )
    noise_moment = lax.dot_general(noise_flat, noise_flat, dims, preferred_element_type=jnp.float32)
    count_column = jnp.full((bands,), count, jnp.float32)
    side = jnp.stack(
        [signal_first, noise_first, count_column, jnp.diagonal(noise_moment)], axis=1
    )
    packed = jnp.tril(signal_moment) + jnp.triu(noise_moment, 1)
    total = total_of(jnp.concatenate([packed, side], axis=1))
    packed_total = total[:, :bands]
    total_side = total[:, bands:]
    below = jnp.tril(packed_total, -1)
    above = jnp.triu(packed_total, 1)
    eye = jnp.eye(bands, dtype=jnp.bool_)
    signal_total = jnp.tril(packed_total) + below.T
    noise_total = jnp.where(eye, total_side[:, 3:4], above + above.T)
    count_total = total_side[0, 2]
    signal_sum = total_side[:, 0]
    inverse_lower, whitened_cov = finish(
        signal_total, noise_total, signal_sum, total_side[:, 1], count_total
    )
    inverse_cast = inverse_lower.astype(jnp.bfloat16)
    mean_signal = signal_sum / count_total
    centered = (
        (weight * (smooth - mean_signal[:, None, None]))
        .astype(jnp.bfloat16)
        .reshape(bands, rows * cols)
    )
    product = jnp.dot(inverse_cast, centered, preferred_element_type=jnp.float32)
    whitened = product.astype(jnp.bfloat16).reshape(bands, rows, cols)
    return (whitened, whitened_cov)


def solution(mesh):
    return jax.shard_map(
        body,
        mesh=mesh,
        in_specs=(P(None, "tile", "group"), P("tile", "group")),
        out_specs=(P(None, "tile", "group"), P()),
        check_vma=False,
    )
```

```python
import jax
import jax.numpy as jnp
from jax import lax
from jax.experimental import pallas as pl
from jax.experimental.pallas import tpu as pltpu
from jax.sharding import PartitionSpec as P

F32 = jnp.float32
BF16 = jnp.bfloat16
VMEM_SPEC = pl.BlockSpec(memory_space=pltpu.VMEM)
GROUP = 8
TAPS = (0.0625, 0.25, 0.375, 0.25, 0.0625)


def flat_pairs(sizes, move):
    y_size, z_size, x_size = sizes
    pairs = []
    for y in range(y_size):
        for core in range(2):
            for z in range(z_size):
                for x in range(x_size):
                    y2, core2, z2, x2 = move(y, core, z, x)
                    source = ((y * 2 + core) * z_size + z) * x_size + x
                    target = ((y2 * 2 + core2) * z_size + z2) * x_size + x2
                    pairs.append((source, target))
    return pairs


SIZES = (4, 8, 4)
CORE_SWAP = flat_pairs(SIZES, lambda y, c, z, x: (y, 1 - c, z, x))
STAGES = (
    [flat_pairs(SIZES, lambda y, c, z, x, k=k: (y, c, z, x ^ k)) for k in (1, 2, 3)],
    [flat_pairs(SIZES, lambda y, c, z, x, k=k: (y ^ k, c, z, x)) for k in (1, 2, 3)],
    [flat_pairs(SIZES, lambda y, c, z, x, k=k: (y, c, z ^ k, x)) for k in (1, 2, 3)],
    [flat_pairs(SIZES, lambda y, c, z, x: (y, c, 7 - z, x))],
)
AXES = ("group", "tile")


def total_of(value):
    half = value.shape[0] // 2
    core = lax.axis_index("group") % 2
    own = lax.dynamic_slice_in_dim(value, core * half, half, axis=0)
    other = lax.dynamic_slice_in_dim(value, (1 - core) * half, half, axis=0)
    own = own + lax.ppermute(other, AXES, CORE_SWAP)
    for stage in STAGES:
        parts = [lax.ppermute(own, AXES, pairs) for pairs in stage]
        if len(parts) == 1:
            own = own + parts[0]
        else:
            own = (own + parts[0]) + (parts[1] + parts[2])
    other = lax.ppermute(own, AXES, CORE_SWAP)
    first = core == 0
    return jnp.concatenate(
        [jnp.where(first, own, other), jnp.where(first, other, own)], axis=0
    )


def split_three(value):
    first = value.astype(jnp.bfloat16)
    rest = value - first.astype(jnp.float32)
    second = rest.astype(jnp.bfloat16)
    third = (rest - second.astype(jnp.float32)).astype(jnp.bfloat16)
    return (first, second, third)


def params(mebibytes):
    return pltpu.CompilerParams(vmem_limit_bytes=mebibytes << 20)


def cost(flops, bytes_accessed):
    return pl.CostEstimate(flops=flops, bytes_accessed=bytes_accessed, transcendentals=0)


def edges_kernel(top_ref, low_ref, first_ref, last_ref):
    first_ref[...] = jnp.swapaxes(top_ref[...], 0, 1)[:2]
    last_ref[...] = jnp.swapaxes(low_ref[...], 0, 1)[14:]


def edge_rows(x):
    bands, rows, cols = x.shape
    shape = jax.ShapeDtypeStruct((2, bands, cols), BF16)
    whole = pl.BlockSpec((2, bands, cols), lambda i: (0, 0, 0))
    return pl.pallas_call(
        edges_kernel,
        grid=(1,),
        out_shape=(shape, shape),
        in_specs=[
            pl.BlockSpec((bands, 16, cols), lambda i: (0, 0, 0)),
            pl.BlockSpec((bands, 16, cols), lambda i: (0, rows // 16 - 1, 0)),
        ],
        out_specs=(whole, whole),
        compiler_params=params(6),
        cost_estimate=cost(0, 4 * bands * 16 * cols),
        name="edge_rows",
    )(x, x)


def rows_first_kernel(x_ref, out_ref):
    out_ref[...] = jnp.swapaxes(x_ref[...], 0, 1)


def rows_first(x):
    bands, rows, cols = x.shape
    return pl.pallas_call(
        rows_first_kernel,
        grid=(rows // 16,),
        out_shape=jax.ShapeDtypeStruct((rows, bands, cols), BF16),
        in_specs=[pl.BlockSpec((bands, 16, cols), lambda i: (0, i, 0))],
        out_specs=pl.BlockSpec((16, bands, cols), lambda i: (i, 0, 0)),
        compiler_params=params(8),
        cost_estimate=cost(0, 4 * bands * rows * cols),
        name="rows_first",
    )(x)


def fold(moment, columns):
    size = moment.shape[0]
    half = size // 2
    wide = moment if moment.shape[1] == 256 else jnp.concatenate(
        [moment, jnp.zeros((size, 256 - size), F32)], axis=1
    )
    row = lax.broadcasted_iota(jnp.int32, (half, 256), 0)
    lane = lax.broadcasted_iota(jnp.int32, (half, 256), 1)
    moved = pltpu.roll(wide[:half], half + 1, 1)
    out = jnp.where(lane <= half + row, wide[half:], moved)
    for place, column in enumerate(columns):
        out = jnp.where(lane == size + 2 + place, column, out)
    return out


def unfold(folded):
    half = folded.shape[0]
    size = 2 * half
    row = lax.broadcasted_iota(jnp.int32, (half, 256), 0)
    lane = lax.broadcasted_iota(jnp.int32, (half, 256), 1)
    back = pltpu.roll(folded, 256 - half - 1, 1)
    upper = jnp.where((lane >= row) & (lane < half), back, 0.0)
    lower = jnp.where(lane <= half + row, folded, 0.0)
    part = jnp.concatenate([upper, lower], axis=0)
    turned = jnp.concatenate([part, jnp.zeros((256 - size, 256), F32)], axis=0).T[:size]
    row = lax.broadcasted_iota(jnp.int32, (size, 256), 0)
    lane = lax.broadcasted_iota(jnp.int32, (size, 256), 1)
    return part + jnp.where(row == lane, 0.0, turned)


def noise_kernel(xt_ref, up_ref, down_ref, weight_ref, out_ref, moment_ref, first_ref):
    rows, bands, cols = xt_ref.shape
    groups = rows // GROUP
    moment_ref[...] = jnp.zeros_like(moment_ref)
    first_ref[...] = jnp.zeros_like(first_ref)

    def step(weights, field):
        parts = []
        total = None
        for i in range(GROUP):
            value = field[i + 1] - 0.5 * (field[i] + field[i + 2])
            value = value * weights[i : i + 1, :]
            total = value if total is None else total + value
            parts.append(value.astype(BF16))
        first_ref[...] += total
        flat = jnp.concatenate(parts, axis=1)
        moment_ref[...] += lax.dot_general(
            flat, flat, (((1,), (1,)), ((), ())), preferred_element_type=F32
        )

    def weights_of(g):
        return weight_ref[pl.ds(pl.multiple_of(g * GROUP, GROUP), GROUP), :].astype(F32)

    def load(r):
        return xt_ref[r].astype(F32)

    step(weights_of(0), [up_ref[1].astype(F32)] + [load(r) for r in range(GROUP + 1)])

    @pl.loop(1, groups - 1)
    def _(g):
        step(weights_of(g), [load(g * GROUP + i - 1) for i in range(GROUP + 2)])

    base = rows - GROUP
    step(
        weights_of(groups - 1),
        [load(base + i - 1) for i in range(GROUP + 1)] + [down_ref[0].astype(F32)],
    )
    first = jnp.sum(first_ref[...], axis=1, keepdims=True)
    count = jnp.sum(weight_ref[...].astype(F32), keepdims=True)
    half = bands // 2
    out_ref[...] = fold(moment_ref[...], [first[:half], first[half:], count])


def noise_moments(xt, up, down, weight):
    rows, bands, cols = xt.shape
    return pl.pallas_call(
        noise_kernel,
        out_shape=jax.ShapeDtypeStruct((bands // 2, 256), F32),
        in_specs=[VMEM_SPEC] * 4,
        out_specs=VMEM_SPEC,
        scratch_shapes=[pltpu.VMEM((bands, bands), F32), pltpu.VMEM((bands, cols), F32)],
        compiler_params=params(6),
        cost_estimate=cost(2 * bands * bands * rows * cols, 2 * bands * rows * cols),
        name="noise_moments",
    )(xt, up, down, weight)


def side_columns_kernel(xt_ref, up_ref, down_ref, out_ref):
    rows, bands, cols = xt_ref.shape
    groups = rows // GROUP
    place = lax.broadcasted_iota(jnp.int32, (GROUP * cols, 128), 0)
    lane = lax.broadcasted_iota(jnp.int32, (GROUP * cols, 128), 1)
    pixel_row, col = place // cols, place % cols
    wanted_low = 2 * pixel_row + col
    wanted_high = 2 * GROUP + 2 * pixel_row + (col - (cols - 2))
    pick = ((col < 2) & (lane == wanted_low)) | ((col >= cols - 2) & (lane == wanted_high))
    pick = jnp.where(pick, 1.0, 0.0).astype(BF16)
    zero = jnp.zeros((bands, cols), BF16)
    sums = [[jnp.zeros((bands, 128), F32) for _ in range(2)] for _ in range(2)]
    lane = lax.broadcasted_iota(jnp.int32, (bands, 128), 1)
    for g in range(groups + 1):
        if g < groups:
            pieces = [xt_ref[g * GROUP + i] for i in range(GROUP)]
        else:
            pieces = [up_ref[0], up_ref[1], down_ref[0], down_ref[1]] + [zero] * 4
        got = jnp.dot(jnp.concatenate(pieces, axis=1), pick, preferred_element_type=F32)
        shift = 16 * (g % 8)
        low = jnp.where(lane < 16, got, 0.0)
        high = jnp.where((lane >= 16) & (lane < 32), got, 0.0)
        chunk = g // 8
        sums[0][chunk] += pltpu.roll(low, shift, 1) if shift else low
        turn = (shift - 16) % 128
        sums[1][chunk] += pltpu.roll(high, turn, 1) if turn else high
    for side in range(2):
        out_ref[side] = jnp.concatenate(sums[side], axis=1).astype(BF16)


def side_columns(xt, up, down):
    rows, bands, cols = xt.shape
    return pl.pallas_call(
        side_columns_kernel,
        out_shape=jax.ShapeDtypeStruct((2, bands, 256), BF16),
        in_specs=[VMEM_SPEC] * 3,
        out_specs=VMEM_SPEC,
        compiler_params=params(8),
        cost_estimate=cost(2 * bands * rows * cols * 32, 2 * bands * rows * cols),
        name="side_columns",
    )(xt, up, down)


def signal_kernel(
    xt_ref, up_ref, down_ref, low_ref, high_ref, weight_ref,
    smooth_ref, out_ref, col_ref, moment_ref, first_ref,
):
    rows, bands, cols = xt_ref.shape
    groups = rows // GROUP
    moment_ref[...] = jnp.zeros_like(moment_ref)
    first_ref[...] = jnp.zeros_like(first_ref)

    def taps_of(distance):
        out = jnp.zeros(distance.shape, F32)
        for k, tap in enumerate(TAPS):
            out = jnp.where(distance == k - 2, tap, out)
        return out

    source = lax.broadcasted_iota(jnp.int32, (2 * cols, 2 * cols), 0)
    target = lax.broadcasted_iota(jnp.int32, (2 * cols, 2 * cols), 1)
    band = jnp.where(
        source // cols == target // cols, taps_of(source % cols - target % cols), 0.0
    ).astype(BF16)
    source = lax.broadcasted_iota(jnp.int32, (128, 2 * cols), 0)
    target = lax.broadcasted_iota(jnp.int32, (128, 2 * cols), 1)
    is_low = source < 16
    pixel_row = (source % 16) // 2
    position = jnp.where(is_low, source % 2 - 2, cols + source % 2)
    sides = []
    for q in range(4):
        keep = (source < 32) & (pixel_row == 2 * q + target // cols)
        sides.append(jnp.where(keep, taps_of(position - target % cols), 0.0).astype(BF16))
    lane = lax.broadcasted_iota(jnp.int32, (bands, 128), 1)

    def side_lanes(chunk, shift):
        low = low_ref[:, 128 * chunk : 128 * chunk + 128].astype(F32)
        high = high_ref[:, 128 * chunk : 128 * chunk + 128].astype(F32)
        low = pltpu.roll(low, (128 - shift) % 128, 1)
        high = pltpu.roll(high, (128 + 16 - shift) % 128, 1)
        return jnp.where(lane < 16, low, jnp.where(lane < 32, high, 0.0)).astype(BF16)

    def smooth_pair(one, two, extra, q):
        pair = jnp.concatenate([one, two], axis=1)
        out = jnp.dot(pair, band, preferred_element_type=F32)
        out += jnp.dot(extra, sides[q], preferred_element_type=F32)
        return (out[:, :cols], out[:, cols:])

    for g in range(groups):
        extra = side_lanes(g // 8, 16 * (g % 8))
        for q in range(4):
            r = g * GROUP + 2 * q
            one, two = smooth_pair(xt_ref[r], xt_ref[r + 1], extra, q)
            col_ref[r + 2] = one
            col_ref[r + 3] = two
    extra = side_lanes(groups // 8, 16 * (groups % 8))
    col_ref[0], col_ref[1] = smooth_pair(up_ref[0], up_ref[1], extra, 0)
    col_ref[rows + 2], col_ref[rows + 3] = smooth_pair(down_ref[0], down_ref[1], extra, 1)

    @pl.loop(0, groups)
    def _(g):
        base = pl.multiple_of(g * GROUP, GROUP)
        weights = weight_ref[pl.ds(base, GROUP), :].astype(F32)
        field = [col_ref[base + i] for i in range(GROUP + 4)]
        parts = []
        total = None
        for i in range(GROUP):
            value = (
                0.0625 * (field[i] + field[i + 4])
                + 0.25 * (field[i + 1] + field[i + 3])
                + 0.375 * field[i + 2]
            )
            smooth_ref[base + i] = value
            value = value * weights[i : i + 1, :]
            total = value if total is None else total + value
            parts.append(value.astype(BF16))
        first_ref[...] += total
        flat = jnp.concatenate(parts, axis=1)
        moment_ref[...] += lax.dot_general(
            flat, flat, (((1,), (1,)), ((), ())), preferred_element_type=F32
        )

    first = jnp.sum(first_ref[...], axis=1, keepdims=True)
    count = jnp.sum(weight_ref[...].astype(F32), keepdims=True)
    half = bands // 2
    out_ref[...] = fold(moment_ref[...], [first[:half], first[half:], count])


def signal_moments(xt, up, down, low, high, weight):
    rows, bands, cols = xt.shape
    return pl.pallas_call(
        signal_kernel,
        out_shape=(
            jax.ShapeDtypeStruct((rows, bands, cols), F32),
            jax.ShapeDtypeStruct((bands // 2, 256), F32),
        ),
        in_specs=[VMEM_SPEC] * 6,
        out_specs=(VMEM_SPEC, VMEM_SPEC),
        scratch_shapes=[
            pltpu.VMEM((rows + 4, bands, cols), F32),
            pltpu.VMEM((bands, bands), F32),
            pltpu.VMEM((bands, cols), F32),
        ],
        compiler_params=params(20),
        cost_estimate=cost(4 * bands * bands * rows * cols, 6 * bands * rows * cols),
        name="signal_moments",
    )(xt, up, down, low, high, weight)


def sums_of(folded):
    size = 2 * folded.shape[0]
    first = jnp.concatenate(
        [folded[:, size + 2 : size + 3], folded[:, size + 3 : size + 4]], axis=0
    )
    return (first, folded[:1, size + 4 : size + 5])


def covariance_of(folded):
    size = 2 * folded.shape[0]
    first, count = sums_of(folded)
    down = jnp.broadcast_to(first, (size, 256))
    across = jnp.concatenate([down, jnp.zeros((256 - size, 256), F32)], axis=0).T[:size]
    return (unfold(folded) - down * across / count) / (count - 1.0)


def whiten_kernel(inverse_ref, sums_ref, weight_ref, smooth_ref, out_ref):
    step_rows, bands, cols = smooth_ref.shape
    weights = weight_ref[...].astype(F32)
    first, count = sums_of(sums_ref[...])
    mean = jnp.broadcast_to(first / count, (bands, cols))
    inverse = inverse_ref[...]
    parts = []
    for pair in range(step_rows // 2):
        pieces = []
        for i in (2 * pair, 2 * pair + 1):
            pieces.append((weights[i : i + 1, :] * (smooth_ref[i] - mean)).astype(BF16))
        product = jnp.dot(inverse, jnp.concatenate(pieces, axis=1), preferred_element_type=F32)
        product = product.astype(BF16)
        parts += [product[None, :, :cols], product[None, :, cols:]]
    out_ref[...] = jnp.swapaxes(jnp.concatenate(parts, axis=0), 0, 1)


def whiten(inverse, sums, weight, smooth):
    rows, bands, cols = smooth.shape
    return pl.pallas_call(
        whiten_kernel,
        grid=(rows // 16,),
        out_shape=jax.ShapeDtypeStruct((bands, rows, cols), BF16),
        in_specs=[
            pl.BlockSpec((bands, bands), lambda i: (0, 0)),
            pl.BlockSpec((bands // 2, 256), lambda i: (0, 0)),
            pl.BlockSpec((16, cols), lambda i: (i, 0)),
            pl.BlockSpec((16, bands, cols), lambda i: (i, 0, 0)),
        ],
        out_specs=pl.BlockSpec((bands, 16, cols), lambda i: (0, i, 0)),
        compiler_params=params(12),
        cost_estimate=cost(2 * bands * bands * rows * cols, 6 * bands * rows * cols),
        name="whiten",
    )(inverse, sums, weight, smooth)


def inverse_factor_kernel(sums_ref, out_ref, cast_ref, work_ref):
    size = out_ref.shape[0]
    width = work_ref.shape[1]
    sub = lax.broadcasted_iota(jnp.int32, (8, 128), 0)
    lane = lax.broadcasted_iota(jnp.int32, (8, width), 1)
    sub_wide = lax.broadcasted_iota(jnp.int32, (8, width), 0)
    work_ref[...] = covariance_of(sums_ref[...])
    for block in range(size // 8):
        base, low = 8 * block, 8 * block + 8
        panel = work_ref[base:low, :]
        cols = [
            jnp.broadcast_to(panel[:, base + j : base + j + 1], (8, 128)) for j in range(8)
        ]
        eye = jnp.where(lane - base == sub_wide, 1.0, 0.0)
        rows = jnp.where((lane >= base) & (lane < low), eye, panel)
        scale = jnp.zeros((8, 128), jnp.float32)
        for j in range(8):
            root = lax.rsqrt(jnp.broadcast_to(cols[j][j : j + 1, :], (8, 128)))
            scale = jnp.where(sub == j, root, scale)
            if j < 7:
                ratio = jnp.where(sub > j, cols[j] * (root * root), 0.0)
                for i in range(j + 1, 8):
                    cols[i] = cols[i] - ratio * jnp.broadcast_to(cols[i][j : j + 1, :], (8, 128))
                ratio_wide = jnp.concatenate([ratio, ratio], axis=1)
                rows = rows - ratio_wide * jnp.broadcast_to(rows[j : j + 1, :], (8, width))
        rows = rows * jnp.concatenate([scale, scale], axis=1)
        work_ref[base:low, :] = jnp.where(lane < low, rows, 0.0)
        if low < size:
            one, two, three = split_three(rows)
            left = jnp.concatenate([one, one, two, two, one, three], axis=0)
            right = jnp.concatenate([one, two, one, two, three, one], axis=0)
            update = lax.dot_general(
                left, right, (((0,), (0,)), ((), ())), preferred_element_type=jnp.float32
            )
            rest = work_ref[low:size, :]
            rest_lane = lax.broadcasted_iota(jnp.int32, rest.shape, 1)
            rest = jnp.where((rest_lane >= base) & (rest_lane < low), 0.0, rest)
            work_ref[low:size, :] = rest - update[low:size, :]
    out_ref[...] = work_ref[:, :size]
    cast_ref[...] = work_ref[:, :size].astype(BF16)


def inverse_factor(sums):
    size = 2 * sums.shape[0]
    return pl.pallas_call(
        inverse_factor_kernel,
        out_shape=(
            jax.ShapeDtypeStruct((size, size), F32),
            jax.ShapeDtypeStruct((size, size), BF16),
        ),
        in_specs=[VMEM_SPEC],
        out_specs=(VMEM_SPEC, VMEM_SPEC),
        scratch_shapes=[pltpu.VMEM((size, 256), F32)],
        compiler_params=params(6),
        cost_estimate=cost(2 * size**3, 8 * size**2),
        name="inverse_factor",
    )(sums)


def whitened_cov_kernel(inverse_ref, sums_ref, out_ref):
    size = inverse_ref.shape[0]
    cov = covariance_of(sums_ref[...])[:, :size]
    inverse = inverse_ref[...]
    left = jnp.dot(inverse, cov, precision=lax.Precision.HIGHEST, preferred_element_type=F32)
    out_ref[...] = lax.dot_general(
        left, inverse, (((1,), (1,)), ((), ())),
        precision=lax.Precision.HIGHEST, preferred_element_type=F32,
    )


def whitened_cov_of(inverse, sums):
    size = inverse.shape[0]
    return pl.pallas_call(
        whitened_cov_kernel,
        out_shape=jax.ShapeDtypeStruct((size, size), F32),
        in_specs=[VMEM_SPEC, VMEM_SPEC],
        out_specs=VMEM_SPEC,
        compiler_params=params(6),
        cost_estimate=cost(24 * size**3, 12 * size**2),
        name="whitened_cov",
    )(inverse, sums)


def line(count):
    forward = [(i, i + 1) for i in range(count - 1)]
    return (forward, [(target, source) for source, target in forward])


def body(radiance, valid_mask):
    first, last = edge_rows(radiance)
    forward, backward = line(lax.axis_size("tile"))
    up = lax.ppermute(last, "tile", forward)
    down = lax.ppermute(first, "tile", backward)
    xt = rows_first(radiance)
    noise = noise_moments(xt, up, down, valid_mask)
    columns = side_columns(xt, up, down)
    forward, backward = line(lax.axis_size("group"))
    low = lax.ppermute(columns[1], "group", forward)
    high = lax.ppermute(columns[0], "group", backward)
    smooth, signal = signal_moments(xt, up, down, low, high, valid_mask)
    noise_total = total_of(noise)
    signal_total = total_of(signal)
    inverse, inverse_cast = inverse_factor(noise_total)
    whitened = whiten(inverse_cast, signal_total, valid_mask, smooth)
    return (whitened, whitened_cov_of(inverse, signal_total))


def solution(mesh):
    return jax.shard_map(
        body,
        mesh=mesh,
        in_specs=(P(None, "tile", "group"), P("tile", "group")),
        out_specs=(P(None, "tile", "group"), P()),
        check_vma=False,
    )
```

```python
import jax
import jax.numpy as jnp
from jax import lax
from jax.experimental import pallas as pl
from jax.experimental.pallas import tpu as pltpu
from jax.sharding import PartitionSpec as P

F32 = jnp.float32
BF16 = jnp.bfloat16
VMEM_SPEC = pl.BlockSpec(memory_space=pltpu.VMEM)
HBM_SPEC = pl.BlockSpec(memory_space=pltpu.HBM)
GROUP = 8
CORNER_GROUP = 12
PIVOTS = 16
TAPS = (0.0625, 0.25, 0.375, 0.25, 0.0625)


def flat_pairs(sizes, move):
    y_size, z_size, x_size = sizes
    pairs = []
    for y in range(y_size):
        for core in range(2):
            for z in range(z_size):
                for x in range(x_size):
                    y2, core2, z2, x2 = move(y, core, z, x)
                    source = ((y * 2 + core) * z_size + z) * x_size + x
                    target = ((y2 * 2 + core2) * z_size + z2) * x_size + x2
                    pairs.append((source, target))
    return pairs


SIZES = (4, 8, 4)
CORE_SWAP = flat_pairs(SIZES, lambda y, c, z, x: (y, 1 - c, z, x))
X_PAIRS = [flat_pairs(SIZES, lambda y, c, z, x, k=k: (y, c, z, x ^ k)) for k in (1, 2, 3)]
STAGES = (
    [flat_pairs(SIZES, lambda y, c, z, x, k=k: (y ^ k, c, z, x)) for k in (1, 2, 3)],
    [flat_pairs(SIZES, lambda y, c, z, x, k=k: (y, c, z ^ k, x)) for k in (1, 2, 3)],
    [flat_pairs(SIZES, lambda y, c, z, x: (y, c, 7 - z, x))],
)
AXES = ("group", "tile")


def total_of(value):
    half = value.shape[1] // 2
    core = lax.axis_index("group") % 2
    x = lax.axis_index("tile") % 4
    own = lax.dynamic_slice_in_dim(value, core * half, half, axis=1)
    other = lax.dynamic_slice_in_dim(value, (1 - core) * half, half, axis=1)
    mine = own + lax.ppermute(other, AXES, CORE_SWAP)

    def block(index):
        return lax.dynamic_index_in_dim(mine, index, axis=0, keepdims=False)

    parts = [lax.ppermute(block(x ^ k), AXES, X_PAIRS[k - 1]) for k in (1, 2, 3)]
    piece = (block(x) + parts[0]) + (parts[1] + parts[2])
    for stage in STAGES:
        parts = [lax.ppermute(piece, AXES, pairs) for pairs in stage]
        if len(parts) == 1:
            piece = piece + parts[0]
        else:
            piece = (piece + parts[0]) + (parts[1] + parts[2])
    got = [piece] + [lax.ppermute(piece, AXES, pairs) for pairs in X_PAIRS]
    blocks = []
    for place in range(4):
        value = got[3]
        for k in (0, 1, 2):
            value = jnp.where(x == place ^ k, got[k], value)
        blocks.append(value)
    mine = jnp.stack(blocks)
    other = lax.ppermute(mine, AXES, CORE_SWAP)
    first = core == 0
    return jnp.concatenate([jnp.where(first, mine, other), jnp.where(first, other, mine)], axis=1)


def split_three(value):
    first = value.astype(jnp.bfloat16)
    rest = value - first.astype(jnp.float32)
    second = rest.astype(jnp.bfloat16)
    third = (rest - second.astype(jnp.float32)).astype(jnp.bfloat16)
    return (first, second, third)


def params(mebibytes):
    return pltpu.CompilerParams(vmem_limit_bytes=mebibytes << 20)


def cost(flops, bytes_accessed):
    return pl.CostEstimate(flops=flops, bytes_accessed=bytes_accessed, transcendentals=0)


def in_hbm(value):
    return pltpu.with_memory_space_constraint(value, pltpu.HBM)


def in_vmem(value):
    return pltpu.with_memory_space_constraint(value, pltpu.VMEM)


def edges_kernel(x_ref, first_ref, last_ref, slab_ref, sems):
    rows = x_ref.shape[1]
    top = pltpu.make_async_copy(x_ref.at[:, pl.ds(0, 16), :], slab_ref.at[0], sems.at[0])
    low = pltpu.make_async_copy(x_ref.at[:, pl.ds(rows - 16, 16), :], slab_ref.at[1], sems.at[1])
    top.start()
    low.start()
    top.wait()
    first_ref[...] = jnp.swapaxes(slab_ref[0], 0, 1)[:2]
    low.wait()
    last_ref[...] = jnp.swapaxes(slab_ref[1], 0, 1)[14:]


def edge_rows(x):
    bands, rows, cols = x.shape
    shape = jax.ShapeDtypeStruct((2, bands, cols), BF16)
    return pl.pallas_call(
        edges_kernel,
        out_shape=(shape, shape),
        in_specs=[HBM_SPEC],
        out_specs=(VMEM_SPEC, VMEM_SPEC),
        scratch_shapes=[pltpu.VMEM((2, bands, 16, cols), BF16), pltpu.SemaphoreType.DMA((2,))],
        compiler_params=params(8),
        cost_estimate=cost(0, 4 * bands * 16 * cols),
        name="edge_rows",
    )(in_hbm(x))


def side_picker(cols):
    place = lax.broadcasted_iota(jnp.int32, (GROUP * cols, 128), 0)
    lane = lax.broadcasted_iota(jnp.int32, (GROUP * cols, 128), 1)
    pixel_row, col = place // cols, place % cols
    wanted_low = 2 * pixel_row + col
    wanted_high = 2 * GROUP + 2 * pixel_row + (col - (cols - 2))
    pick = ((col < 2) & (lane == wanted_low)) | ((col >= cols - 2) & (lane == wanted_high))
    return jnp.where(pick, 1.0, 0.0).astype(BF16)


def side_lanes_of(pieces, pick, g):
    got = jnp.dot(jnp.concatenate(pieces, axis=1), pick, preferred_element_type=F32)
    lane = lax.broadcasted_iota(jnp.int32, got.shape, 1)
    shift = 16 * (g % 8)
    turn = (shift - 16) % 128
    low = jnp.where(lane < 16, got, 0.0)
    high = jnp.where((lane >= 16) & (lane < 32), got, 0.0)
    return (
        pltpu.roll(low, shift, 1) if shift else low,
        pltpu.roll(high, turn, 1) if turn else high,
    )


def rows_first_kernel(x_ref, out_ref, side_ref, slab_ref, turned_ref, in_sems, out_sems):
    slabs, bands, _, cols = slab_ref.shape
    inward = [
        pltpu.make_async_copy(x_ref.at[:, pl.ds(16 * s, 16), :], slab_ref.at[s], in_sems.at[s])
        for s in range(slabs)
    ]
    outward = [
        pltpu.make_async_copy(
            turned_ref.at[pl.ds(16 * s, 16)], out_ref.at[pl.ds(16 * s, 16)], out_sems.at[s]
        )
        for s in range(slabs)
    ]
    for copy in inward:
        copy.start()
    pick = side_picker(cols)
    sums = [[jnp.zeros((bands, 128), F32) for _ in range(2)] for _ in range(2)]
    for s in range(slabs):
        inward[s].wait()
        turned_ref[16 * s : 16 * s + 16] = jnp.swapaxes(slab_ref[s], 0, 1)
        outward[s].start()
        for g in (2 * s, 2 * s + 1):
            pieces = [turned_ref[g * GROUP + i] for i in range(GROUP)]
            low, high = side_lanes_of(pieces, pick, g)
            sums[0][g // 8] += low
            sums[1][g // 8] += high
    for side in range(2):
        side_ref[side] = jnp.concatenate(sums[side], axis=1).astype(BF16)
    for copy in outward:
        copy.wait()


def rows_first(x):
    bands, rows, cols = x.shape
    slabs = rows // 16
    return pl.pallas_call(
        rows_first_kernel,
        out_shape=(
            pltpu.HBM((rows, bands, cols), BF16),
            jax.ShapeDtypeStruct((2, bands, 256), BF16),
        ),
        in_specs=[HBM_SPEC],
        out_specs=(HBM_SPEC, VMEM_SPEC),
        scratch_shapes=[
            pltpu.VMEM((slabs, bands, 16, cols), BF16),
            pltpu.VMEM((rows, bands, cols), BF16),
            pltpu.SemaphoreType.DMA((slabs,)),
            pltpu.SemaphoreType.DMA((slabs,)),
        ],
        compiler_params=params(20),
        cost_estimate=cost(2 * bands * rows * cols * 32, 4 * bands * rows * cols),
        name="rows_first",
    )(in_hbm(x))


def corners_kernel(side_ref, up_ref, down_ref, low_ref, high_ref):
    bands, cols = up_ref.shape[1:]
    zero = jnp.zeros((bands, cols), BF16)
    pieces = [up_ref[0], up_ref[1], down_ref[0], down_ref[1]] + [zero] * 4
    parts = side_lanes_of(pieces, side_picker(cols), CORNER_GROUP)
    for side, out_ref in ((0, low_ref), (1, high_ref)):
        out_ref[:, :128] = side_ref[side][:, :128]
        out_ref[:, 128:] = (side_ref[side][:, 128:].astype(F32) + parts[side]).astype(BF16)


def side_columns(side, up, down):
    bands = side.shape[1]
    shape = jax.ShapeDtypeStruct((bands, 256), BF16)
    return pl.pallas_call(
        corners_kernel,
        out_shape=(shape, shape),
        in_specs=[VMEM_SPEC] * 3,
        out_specs=(VMEM_SPEC, VMEM_SPEC),
        compiler_params=params(8),
        cost_estimate=cost(2 * bands * 1024 * 128, 6 * bands * 256),
        name="side_columns",
    )(side, up, down)


def group_copy(source_ref, target_ref, sems, g):
    start = g * GROUP if isinstance(g, int) else pl.multiple_of(g * GROUP, GROUP)
    window = pl.ds(start, GROUP)
    return pltpu.make_async_copy(source_ref.at[window], target_ref.at[window], sems.at[g])


def fold(moment, columns):
    size = moment.shape[0]
    half = size // 2
    wide = moment if moment.shape[1] == 256 else jnp.concatenate(
        [moment, jnp.zeros((size, 256 - size), F32)], axis=1
    )
    row = lax.broadcasted_iota(jnp.int32, (half, 256), 0)
    lane = lax.broadcasted_iota(jnp.int32, (half, 256), 1)
    moved = pltpu.roll(wide[:half], half + 1, 1)
    out = jnp.where(lane <= half + row, wide[half:], moved)
    for place, column in enumerate(columns):
        out = jnp.where(lane == size + 2 + place, column, out)
    return out


def unfold(folded):
    half = folded.shape[0]
    size = 2 * half
    row = lax.broadcasted_iota(jnp.int32, (half, 256), 0)
    lane = lax.broadcasted_iota(jnp.int32, (half, 256), 1)
    back = pltpu.roll(folded, 256 - half - 1, 1)
    upper = jnp.where((lane >= row) & (lane < half), back, 0.0)
    lower = jnp.where(lane <= half + row, folded, 0.0)
    part = jnp.concatenate([upper, lower], axis=0)
    turned = jnp.concatenate([part, jnp.zeros((256 - size, 256), F32)], axis=0).T[:size]
    row = lax.broadcasted_iota(jnp.int32, (size, 256), 0)
    lane = lax.broadcasted_iota(jnp.int32, (size, 256), 1)
    return part + jnp.where(row == lane, 0.0, turned)


def noise_kernel(xt_ref, up_ref, down_ref, weight_ref, out_ref, moment_ref, first_ref):
    rows, bands, cols = xt_ref.shape
    groups = rows // GROUP
    moment_ref[...] = jnp.zeros_like(moment_ref)
    first_ref[...] = jnp.zeros_like(first_ref)

    def step(weights, field):
        parts = []
        total = None
        for i in range(GROUP):
            value = field[i + 1] - 0.5 * (field[i] + field[i + 2])
            value = value * weights[i : i + 1, :]
            total = value if total is None else total + value
            parts.append(value.astype(BF16))
        first_ref[...] += total
        flat = jnp.concatenate(parts, axis=1)
        moment_ref[...] += lax.dot_general(
            flat, flat, (((1,), (1,)), ((), ())), preferred_element_type=F32
        )

    def weights_of(g):
        return weight_ref[pl.ds(pl.multiple_of(g * GROUP, GROUP), GROUP), :].astype(F32)

    def load(r):
        return xt_ref[r].astype(F32)

    step(weights_of(0), [up_ref[1].astype(F32)] + [load(r) for r in range(GROUP + 1)])

    @pl.loop(1, groups - 1)
    def _(g):
        step(weights_of(g), [load(g * GROUP + i - 1) for i in range(GROUP + 2)])

    base = rows - GROUP
    step(
        weights_of(groups - 1),
        [load(base + i - 1) for i in range(GROUP + 1)] + [down_ref[0].astype(F32)],
    )
    first = jnp.sum(first_ref[...], axis=1, keepdims=True)
    count = jnp.sum(weight_ref[...].astype(F32), keepdims=True)
    half = bands // 2
    folded = fold(moment_ref[...], [first[:half], first[half:], count])
    out_ref[0] = folded[:, :128]
    out_ref[1] = folded[:, 128:]


def noise_moments(xt, up, down, weight):
    rows, bands, cols = xt.shape
    return pl.pallas_call(
        noise_kernel,
        out_shape=jax.ShapeDtypeStruct((2, bands // 2, 128), F32),
        in_specs=[VMEM_SPEC] * 4,
        out_specs=VMEM_SPEC,
        scratch_shapes=[pltpu.VMEM((bands, bands), F32), pltpu.VMEM((bands, cols), F32)],
        compiler_params=params(6),
        cost_estimate=cost(2 * bands * bands * rows * cols, 2 * bands * rows * cols),
        name="noise_moments",
    )(in_vmem(xt), up, down, weight)


def signal_kernel(
    xt_ref, up_ref, down_ref, low_ref, high_ref, weight_ref,
    result_ref, out_ref, col_ref, moment_ref, first_ref, smooth_ref, sems,
):
    rows, bands, cols = xt_ref.shape
    groups = rows // GROUP
    moment_ref[...] = jnp.zeros_like(moment_ref)
    first_ref[...] = jnp.zeros_like(first_ref)

    def taps_of(distance):
        out = jnp.zeros(distance.shape, F32)
        for k, tap in enumerate(TAPS):
            out = jnp.where(distance == k - 2, tap, out)
        return out

    source = lax.broadcasted_iota(jnp.int32, (2 * cols, 2 * cols), 0)
    target = lax.broadcasted_iota(jnp.int32, (2 * cols, 2 * cols), 1)
    band = jnp.where(
        source // cols == target // cols, taps_of(source % cols - target % cols), 0.0
    ).astype(BF16)
    source = lax.broadcasted_iota(jnp.int32, (128, 2 * cols), 0)
    target = lax.broadcasted_iota(jnp.int32, (128, 2 * cols), 1)
    is_low = source < 16
    pixel_row = (source % 16) // 2
    position = jnp.where(is_low, source % 2 - 2, cols + source % 2)
    sides = []
    for q in range(4):
        keep = (source < 32) & (pixel_row == 2 * q + target // cols)
        sides.append(jnp.where(keep, taps_of(position - target % cols), 0.0).astype(BF16))
    lane = lax.broadcasted_iota(jnp.int32, (bands, 128), 1)

    def side_lanes(chunk, shift):
        low = low_ref[:, 128 * chunk : 128 * chunk + 128].astype(F32)
        high = high_ref[:, 128 * chunk : 128 * chunk + 128].astype(F32)
        low = pltpu.roll(low, (128 - shift) % 128, 1)
        high = pltpu.roll(high, (128 + 16 - shift) % 128, 1)
        return jnp.where(lane < 16, low, jnp.where(lane < 32, high, 0.0)).astype(BF16)

    def smooth_pair(one, two, extra, q):
        pair = jnp.concatenate([one, two], axis=1)
        out = jnp.dot(pair, band, preferred_element_type=F32)
        out += jnp.dot(extra, sides[q], preferred_element_type=F32)
        return (out[:, :cols], out[:, cols:])

    def column_pass(g):
        if g < groups:
            extra = side_lanes(g // 8, 16 * (g % 8))
            for q in range(4):
                r = g * GROUP + 2 * q
                one, two = smooth_pair(xt_ref[r], xt_ref[r + 1], extra, q)
                col_ref[r + 2] = one
                col_ref[r + 3] = two
        elif g == groups:
            extra = side_lanes(groups // 8, 16 * (groups % 8))
            one, two = smooth_pair(down_ref[0], down_ref[1], extra, 1)
            col_ref[rows + 2] = one
            col_ref[rows + 3] = two

    def row_pass(g):
        base = g * GROUP
        weights = weight_ref[base : base + GROUP, :].astype(F32)
        field = [col_ref[base + i] for i in range(GROUP + 4)]
        parts = []
        total = None
        for i in range(GROUP):
            value = (
                0.0625 * (field[i] + field[i + 4])
                + 0.25 * (field[i + 1] + field[i + 3])
                + 0.375 * field[i + 2]
            )
            smooth_ref[base + i] = value
            value = value * weights[i : i + 1, :]
            total = value if total is None else total + value
            parts.append(value.astype(BF16))
        group_copy(smooth_ref, result_ref, sems, g).start()
        first_ref[...] += total
        flat = jnp.concatenate(parts, axis=1)
        moment_ref[...] += lax.dot_general(
            flat, flat, (((1,), (1,)), ((), ())), preferred_element_type=F32
        )

    extra = side_lanes(groups // 8, 16 * (groups % 8))
    one, two = smooth_pair(up_ref[0], up_ref[1], extra, 0)
    col_ref[0] = one
    col_ref[1] = two
    column_pass(0)
    column_pass(1)
    for g in range(groups):
        column_pass(g + 2)
        row_pass(g)

    first = jnp.sum(first_ref[...], axis=1, keepdims=True)
    count = jnp.sum(weight_ref[...].astype(F32), keepdims=True)
    half = bands // 2
    folded = fold(moment_ref[...], [first[:half], first[half:], count])
    out_ref[0] = folded[:, :128]
    out_ref[1] = folded[:, 128:]
    for g in range(groups):
        group_copy(smooth_ref, result_ref, sems, g).wait()


def signal_moments(xt, up, down, low, high, weight):
    rows, bands, cols = xt.shape
    return pl.pallas_call(
        signal_kernel,
        out_shape=(
            pltpu.HBM((rows, bands, cols), F32),
            jax.ShapeDtypeStruct((2, bands // 2, 128), F32),
        ),
        in_specs=[VMEM_SPEC] * 6,
        out_specs=(HBM_SPEC, VMEM_SPEC),
        scratch_shapes=[
            pltpu.VMEM((rows + 4, bands, cols), F32),
            pltpu.VMEM((bands, bands), F32),
            pltpu.VMEM((bands, cols), F32),
            pltpu.VMEM((rows, bands, cols), F32),
            pltpu.SemaphoreType.DMA((rows // GROUP,)),
        ],
        compiler_params=params(32),
        cost_estimate=cost(4 * bands * bands * rows * cols, 6 * bands * rows * cols),
        name="signal_moments",
    )(in_vmem(xt), up, down, low, high, weight)


def folded_of(sums_ref, which):
    return jnp.concatenate([sums_ref[2 * which], sums_ref[2 * which + 1]], axis=1)


def sums_of(folded):
    size = 2 * folded.shape[0]
    first = jnp.concatenate(
        [folded[:, size + 2 : size + 3], folded[:, size + 3 : size + 4]], axis=0
    )
    return (first, folded[:1, size + 4 : size + 5])


def covariance_of(folded):
    size = 2 * folded.shape[0]
    first, count = sums_of(folded)
    down = jnp.broadcast_to(first, (size, 256))
    across = jnp.concatenate([down, jnp.zeros((256 - size, 256), F32)], axis=0).T[:size]
    return (unfold(folded) - down * across / count) / (count - 1.0)


def factor_into(work_ref, size):
    width = work_ref.shape[1]
    step = PIVOTS
    sub = lax.broadcasted_iota(jnp.int32, (step, 128), 0)
    lane = lax.broadcasted_iota(jnp.int32, (step, width), 1)
    sub_wide = lax.broadcasted_iota(jnp.int32, (step, width), 0)
    for base in range(0, size, step):
        low = base + step
        panel = work_ref[base:low, :]
        cols = [
            jnp.broadcast_to(panel[:, base + j : base + j + 1], (step, 128)) for j in range(step)
        ]
        eye = jnp.where(lane - base == sub_wide, 1.0, 0.0)
        rows = jnp.where((lane >= base) & (lane < low), eye, panel)
        scale = jnp.zeros((step, 128), F32)
        for j in range(step):
            root = lax.rsqrt(jnp.broadcast_to(cols[j][j : j + 1, :], (step, 128)))
            scale = jnp.where(sub == j, root, scale)
            if j < step - 1:
                ratio = jnp.where(sub > j, cols[j] * (root * root), 0.0)
                for i in range(j + 1, step):
                    cols[i] = cols[i] - ratio * jnp.broadcast_to(
                        cols[i][j : j + 1, :], (step, 128)
                    )
                ratio_wide = jnp.concatenate([ratio, ratio], axis=1)
                rows = rows - ratio_wide * jnp.broadcast_to(rows[j : j + 1, :], (step, width))
        rows = rows * jnp.concatenate([scale, scale], axis=1)
        work_ref[base:low, :] = jnp.where(lane < low, rows, 0.0)
        if low < size:
            cut = 128 if low >= 128 else 0
            one, two, three = split_three(rows)
            left = jnp.concatenate([one, one, two, two, one, three], axis=0)
            right = jnp.concatenate([one, two, one, two, three, one], axis=0)
            update = lax.dot_general(
                left[:, cut:], right, (((0,), (0,)), ((), ())), preferred_element_type=F32
            )
            rest = work_ref[low:size, :]
            rest_lane = lax.broadcasted_iota(jnp.int32, rest.shape, 1)
            rest = jnp.where((rest_lane >= base) & (rest_lane < low), 0.0, rest)
            work_ref[low:size, :] = rest - update[low - cut : size - cut, :]


def finish_kernel(
    sums_ref, weight_ref, field_ref, result_ref, cov_ref,
    work_ref, smooth_ref, out_ref, in_sems, out_sems,
):
    rows, bands, cols = smooth_ref.shape
    groups, slabs = rows // GROUP, rows // 16
    for g in range(groups):
        group_copy(field_ref, smooth_ref, in_sems, g).start()
    work_ref[...] = covariance_of(folded_of(sums_ref, 0))
    factor_into(work_ref, bands)
    inverse = work_ref[:, :bands]
    inverse_cast = inverse.astype(BF16)
    first, count = sums_of(folded_of(sums_ref, 1))
    mean = jnp.broadcast_to(first / count, (bands, cols))

    def outward(s):
        window = pl.ds(16 * s if isinstance(s, int) else pl.multiple_of(16 * s, 16), 16)
        return pltpu.make_async_copy(out_ref.at[s], result_ref.at[:, window, :], out_sems.at[s])

    @pl.loop(0, slabs)
    def _(s):
        base = pl.multiple_of(16 * s, 16)
        weights = weight_ref[pl.ds(base, 16), :].astype(F32)
        parts = []
        for pair in range(8):
            if pair % 4 == 0:
                group_copy(field_ref, smooth_ref, in_sems, 2 * s + pair // 4).wait()
            pieces = []
            for i in (2 * pair, 2 * pair + 1):
                pieces.append((weights[i : i + 1, :] * (smooth_ref[base + i] - mean)).astype(BF16))
            product = jnp.dot(
                inverse_cast, jnp.concatenate(pieces, axis=1), preferred_element_type=F32
            )
            product = product.astype(BF16)
            parts += [product[None, :, :cols], product[None, :, cols:]]
        out_ref[s] = jnp.swapaxes(jnp.concatenate(parts, axis=0), 0, 1)
        outward(s).start()

    cov = covariance_of(folded_of(sums_ref, 1))[:, :bands]
    left = jnp.dot(inverse, cov, precision=lax.Precision.HIGHEST, preferred_element_type=F32)
    cov_ref[...] = lax.dot_general(
        left, inverse, (((1,), (1,)), ((), ())),
        precision=lax.Precision.HIGHEST, preferred_element_type=F32,
    )
    for s in range(slabs):
        outward(s).wait()


def finish(sums, weight, smooth):
    rows, bands, cols = smooth.shape
    groups, slabs = rows // GROUP, rows // 16
    return pl.pallas_call(
        finish_kernel,
        out_shape=(
            pltpu.HBM((bands, rows, cols), BF16),
            jax.ShapeDtypeStruct((bands, bands), F32),
        ),
        in_specs=[VMEM_SPEC, VMEM_SPEC, HBM_SPEC],
        out_specs=(HBM_SPEC, VMEM_SPEC),
        scratch_shapes=[
            pltpu.VMEM((bands, 256), F32),
            pltpu.VMEM((rows, bands, cols), F32),
            pltpu.VMEM((slabs, bands, 16, cols), BF16),
            pltpu.SemaphoreType.DMA((groups,)),
            pltpu.SemaphoreType.DMA((slabs,)),
        ],
        compiler_params=params(36),
        cost_estimate=cost(2 * bands * bands * rows * cols, 6 * bands * rows * cols),
        name="finish",
    )(sums, weight, in_hbm(smooth))


def line(count):
    forward = [(i, i + 1) for i in range(count - 1)]
    return (forward, [(target, source) for source, target in forward])


def body(radiance, valid_mask):
    first, last = edge_rows(radiance)
    forward, backward = line(lax.axis_size("tile"))
    up = lax.ppermute(last, "tile", forward)
    down = lax.ppermute(first, "tile", backward)
    xt, side = rows_first(radiance)
    to_low, to_high = side_columns(side, up, down)
    forward, backward = line(lax.axis_size("group"))
    low = lax.ppermute(to_high, "group", forward)
    high = lax.ppermute(to_low, "group", backward)
    noise = noise_moments(xt, up, down, valid_mask)
    smooth, signal = signal_moments(xt, up, down, low, high, valid_mask)
    sums = total_of(jnp.concatenate([noise, signal], axis=0))
    whitened, whitened_cov = finish(sums, valid_mask, smooth)
    return (whitened, whitened_cov)


def solution(mesh):
    return jax.shard_map(
        body,
        mesh=mesh,
        in_specs=(P(None, "tile", "group"), P("tile", "group")),
        out_specs=(P(None, "tile", "group"), P()),
        check_vma=False,
    )
```

```python
import jax
import jax.numpy as jnp
from jax import lax
from jax.experimental import pallas as pl
from jax.experimental.pallas import tpu as pltpu
from jax.sharding import PartitionSpec as P

F32 = jnp.float32
BF16 = jnp.bfloat16
VMEM_SPEC = pl.BlockSpec(memory_space=pltpu.VMEM)
HBM_SPEC = pl.BlockSpec(memory_space=pltpu.HBM)
GROUP = 8
CORNER_GROUP = 12
PIVOTS = 16
TAPS = (0.0625, 0.25, 0.375, 0.25, 0.0625)


def flat_pairs(sizes, move):
    y_size, z_size, x_size = sizes
    pairs = []
    for y in range(y_size):
        for core in range(2):
            for z in range(z_size):
                for x in range(x_size):
                    y2, core2, z2, x2 = move(y, core, z, x)
                    source = ((y * 2 + core) * z_size + z) * x_size + x
                    target = ((y2 * 2 + core2) * z_size + z2) * x_size + x2
                    pairs.append((source, target))
    return pairs


SIZES = (4, 8, 4)
CORE_SWAP = flat_pairs(SIZES, lambda y, c, z, x: (y, 1 - c, z, x))
STAGES = (
    [flat_pairs(SIZES, lambda y, c, z, x, k=k: (y, c, z, x ^ k)) for k in (1, 2, 3)],
    [flat_pairs(SIZES, lambda y, c, z, x, k=k: (y ^ k, c, z, x)) for k in (1, 2, 3)],
    [flat_pairs(SIZES, lambda y, c, z, x, k=k: (y, c, z ^ k, x)) for k in (1, 2, 3)],
    [flat_pairs(SIZES, lambda y, c, z, x: (y, c, 7 - z, x))],
)
AXES = ("group", "tile")


def total_of(value):
    first = lax.axis_index("group") % 2 == 0
    own = jnp.where(first, value[0], value[1])
    other = jnp.where(first, value[1], value[0])
    own = own + lax.ppermute(other, AXES, CORE_SWAP)
    for stage in STAGES:
        parts = [lax.ppermute(own, AXES, pairs) for pairs in stage]
        if len(parts) == 1:
            own = own + parts[0]
        else:
            own = (own + parts[0]) + (parts[1] + parts[2])
    other = lax.ppermute(own, AXES, CORE_SWAP)
    return jnp.stack([jnp.where(first, own, other), jnp.where(first, other, own)])


def split_three(value):
    first = value.astype(jnp.bfloat16)
    rest = value - first.astype(jnp.float32)
    second = rest.astype(jnp.bfloat16)
    third = (rest - second.astype(jnp.float32)).astype(jnp.bfloat16)
    return (first, second, third)


def params(mebibytes):
    return pltpu.CompilerParams(vmem_limit_bytes=mebibytes << 20)


def cost(flops, bytes_accessed):
    return pl.CostEstimate(flops=flops, bytes_accessed=bytes_accessed, transcendentals=0)


def in_hbm(value):
    return pltpu.with_memory_space_constraint(value, pltpu.HBM)


def in_vmem(value):
    return pltpu.with_memory_space_constraint(value, pltpu.VMEM)


def edges_kernel(x_ref, first_ref, last_ref, slab_ref, sems):
    rows = x_ref.shape[1]
    top = pltpu.make_async_copy(x_ref.at[:, pl.ds(0, 16), :], slab_ref.at[0], sems.at[0])
    low = pltpu.make_async_copy(x_ref.at[:, pl.ds(rows - 16, 16), :], slab_ref.at[1], sems.at[1])
    top.start()
    low.start()
    top.wait()
    first_ref[...] = jnp.swapaxes(slab_ref[0], 0, 1)[:2]
    low.wait()
    last_ref[...] = jnp.swapaxes(slab_ref[1], 0, 1)[14:]


def edge_rows(x):
    bands, rows, cols = x.shape
    shape = jax.ShapeDtypeStruct((2, bands, cols), BF16)
    return pl.pallas_call(
        edges_kernel,
        out_shape=(shape, shape),
        in_specs=[HBM_SPEC],
        out_specs=(VMEM_SPEC, VMEM_SPEC),
        scratch_shapes=[pltpu.VMEM((2, bands, 16, cols), BF16), pltpu.SemaphoreType.DMA((2,))],
        compiler_params=params(8),
        cost_estimate=cost(0, 4 * bands * 16 * cols),
        name="edge_rows",
    )(in_hbm(x))


def side_picker(cols):
    place = lax.broadcasted_iota(jnp.int32, (GROUP * cols, 128), 0)
    lane = lax.broadcasted_iota(jnp.int32, (GROUP * cols, 128), 1)
    pixel_row, col = place // cols, place % cols
    wanted_low = 2 * pixel_row + col
    wanted_high = 2 * GROUP + 2 * pixel_row + (col - (cols - 2))
    pick = ((col < 2) & (lane == wanted_low)) | ((col >= cols - 2) & (lane == wanted_high))
    return jnp.where(pick, 1.0, 0.0).astype(BF16)


def side_lanes_of(pieces, pick, g):
    got = jnp.dot(jnp.concatenate(pieces, axis=1), pick, preferred_element_type=F32)
    lane = lax.broadcasted_iota(jnp.int32, got.shape, 1)
    shift = 16 * (g % 8)
    turn = (shift - 16) % 128
    low = jnp.where(lane < 16, got, 0.0)
    high = jnp.where((lane >= 16) & (lane < 32), got, 0.0)
    return (
        pltpu.roll(low, shift, 1) if shift else low,
        pltpu.roll(high, turn, 1) if turn else high,
    )


def noise_rows(row_of, weight_ref, rows, moment_ref, first_ref):
    parts = []
    total = None
    for r in rows:
        value = row_of(r) - 0.5 * (row_of(r - 1) + row_of(r + 1))
        value = value * weight_ref[r : r + 1, :].astype(F32)
        total = value if total is None else total + value
        parts.append(value.astype(BF16))
    first_ref[...] += total
    flat = jnp.concatenate(parts, axis=1)
    moment_ref[...] += lax.dot_general(
        flat, flat, (((1,), (1,)), ((), ())), preferred_element_type=F32
    )


def rows_first_kernel(
    x_ref, weight_ref, out_ref, side_ref, moment_ref, first_ref,
    slab_ref, turned_ref, in_sems, out_sems,
):
    slabs, bands, _, cols = slab_ref.shape
    rows = 16 * slabs

    def row_of(r):
        return turned_ref[r].astype(F32)

    inward = [
        pltpu.make_async_copy(x_ref.at[:, pl.ds(16 * s, 16), :], slab_ref.at[s], in_sems.at[s])
        for s in range(slabs)
    ]
    due = {begin: range(begin, end) for begin, end in spans_of(slabs)}
    outward = [
        pltpu.make_async_copy(
            turned_ref.at[pl.ds(16 * s, 16)], out_ref.at[pl.ds(16 * s, 16)], out_sems.at[s]
        )
        for s in range(slabs)
    ]
    for copy in inward:
        copy.start()
    moment_ref[...] = jnp.zeros_like(moment_ref)
    first_ref[...] = jnp.zeros_like(first_ref)
    pick = side_picker(cols)
    sums = [[jnp.zeros((bands, 128), F32) for _ in range(2)] for _ in range(2)]
    for s in range(slabs):
        for later in due.get(s, ()):
            inward[later].wait()
        turned_ref[16 * s : 16 * s + 16] = jnp.swapaxes(slab_ref[s], 0, 1)
        outward[s].start()
        for g in (2 * s, 2 * s + 1):
            pieces = [turned_ref[g * GROUP + i] for i in range(GROUP)]
            low, high = side_lanes_of(pieces, pick, g)
            sums[0][g // 8] += low
            sums[1][g // 8] += high
        start = max(16 * s - 7, 1)
        for base in range(start, 16 * s + 15, 8):
            stop = min(base + 8, 16 * s + 9 if s < slabs - 1 else rows - 1)
            if base < stop:
                noise_rows(row_of, weight_ref, range(base, stop), moment_ref, first_ref)
    for side in range(2):
        side_ref[side] = jnp.concatenate(sums[side], axis=1).astype(BF16)
    for copy in outward:
        copy.wait()


def rows_first(x, weight):
    bands, rows, cols = x.shape
    slabs = rows // 16
    return pl.pallas_call(
        rows_first_kernel,
        out_shape=(
            pltpu.HBM((rows, bands, cols), BF16),
            jax.ShapeDtypeStruct((2, bands, 256), BF16),
            jax.ShapeDtypeStruct((bands, bands), F32),
            jax.ShapeDtypeStruct((bands, cols), F32),
        ),
        in_specs=[HBM_SPEC, VMEM_SPEC],
        out_specs=(HBM_SPEC, VMEM_SPEC, VMEM_SPEC, VMEM_SPEC),
        scratch_shapes=[
            pltpu.VMEM((slabs, bands, 16, cols), BF16),
            pltpu.VMEM((rows, bands, cols), BF16),
            pltpu.SemaphoreType.DMA((slabs,)),
            pltpu.SemaphoreType.DMA((slabs,)),
        ],
        compiler_params=params(20),
        cost_estimate=cost(2 * bands * bands * rows * cols, 4 * bands * rows * cols),
        name="rows_first",
    )(in_hbm(x), weight)


def put_folded(out_ref, moment_ref, first_ref, count):
    half = moment_ref.shape[0] // 2
    first = jnp.sum(first_ref[...], axis=1, keepdims=True)
    folded = fold(moment_ref[...], [first[:half], first[half:], count])
    out_ref[0] = folded[:, :128]
    out_ref[1] = folded[:, 128:]


def corners_kernel(
    side_ref, up_ref, down_ref, top_ref, bottom_ref, weight_ref, noise_ref, noise_first_ref,
    low_ref, high_ref, out_ref, moment_ref, first_ref,
):
    bands, cols = up_ref.shape[1:]
    rows = weight_ref.shape[0]
    zero = jnp.zeros((bands, cols), BF16)
    pieces = [up_ref[0], up_ref[1], down_ref[0], down_ref[1]] + [zero] * 4
    parts = side_lanes_of(pieces, side_picker(cols), CORNER_GROUP)
    for side, side_out_ref in ((0, low_ref), (1, high_ref)):
        side_out_ref[:, :128] = side_ref[side][:, :128]
        side_out_ref[:, 128:] = (side_ref[side][:, 128:].astype(F32) + parts[side]).astype(BF16)

    def row_of(r):
        if r < 2:
            row = up_ref[1] if r < 0 else top_ref[r]
        else:
            row = down_ref[0] if r == rows else bottom_ref[r - rows + 2]
        return row.astype(F32)

    moment_ref[...] = noise_ref[...]
    first_ref[...] = noise_first_ref[...]
    noise_rows(row_of, weight_ref, (0, rows - 1), moment_ref, first_ref)
    count = jnp.sum(weight_ref[...].astype(F32), keepdims=True)
    put_folded(out_ref, moment_ref, first_ref, count)


def side_columns(side, up, down, top, bottom, weight, noise, noise_first):
    bands = side.shape[1]
    shape = jax.ShapeDtypeStruct((bands, 256), BF16)
    return pl.pallas_call(
        corners_kernel,
        out_shape=(shape, shape, jax.ShapeDtypeStruct((2, bands // 2, 128), F32)),
        in_specs=[VMEM_SPEC] * 8,
        out_specs=(VMEM_SPEC,) * 3,
        scratch_shapes=[pltpu.VMEM((bands, bands), F32), pltpu.VMEM(noise_first.shape, F32)],
        compiler_params=params(10),
        cost_estimate=cost(2 * bands * 1024 * 128, 6 * bands * 256),
        name="side_columns",
    )(side, up, down, top, bottom, weight, noise, noise_first)


def spans_of(count):
    marks = (0, count // 6, count // 2, count)
    return list(zip(marks[:-1], marks[1:]))


def group_copy(source_ref, target_ref, sems, g):
    start = g * GROUP if isinstance(g, int) else pl.multiple_of(g * GROUP, GROUP)
    window = pl.ds(start, GROUP)
    return pltpu.make_async_copy(source_ref.at[window], target_ref.at[window], sems.at[g])


def fold(moment, columns):
    size = moment.shape[0]
    half = size // 2
    wide = moment if moment.shape[1] == 256 else jnp.concatenate(
        [moment, jnp.zeros((size, 256 - size), F32)], axis=1
    )
    row = lax.broadcasted_iota(jnp.int32, (half, 256), 0)
    lane = lax.broadcasted_iota(jnp.int32, (half, 256), 1)
    moved = pltpu.roll(wide[:half], half + 1, 1)
    out = jnp.where(lane <= half + row, wide[half:], moved)
    for place, column in enumerate(columns):
        out = jnp.where(lane == size + 2 + place, column, out)
    return out


def unfold(folded):
    half = folded.shape[0]
    size = 2 * half
    row = lax.broadcasted_iota(jnp.int32, (half, 256), 0)
    lane = lax.broadcasted_iota(jnp.int32, (half, 256), 1)
    back = pltpu.roll(folded, 256 - half - 1, 1)
    upper = jnp.where((lane >= row) & (lane < half), back, 0.0)
    lower = jnp.where(lane <= half + row, folded, 0.0)
    part = jnp.concatenate([upper, lower], axis=0)
    turned = jnp.concatenate([part, jnp.zeros((256 - size, 256), F32)], axis=0).T[:size]
    row = lax.broadcasted_iota(jnp.int32, (size, 256), 0)
    lane = lax.broadcasted_iota(jnp.int32, (size, 256), 1)
    return part + jnp.where(row == lane, 0.0, turned)


def signal_kernel(
    xt_ref, up_ref, down_ref, low_ref, high_ref, weight_ref,
    result_ref, out_ref, col_ref, moment_ref, first_ref, smooth_ref, sems,
):
    rows, bands, cols = xt_ref.shape
    groups = rows // GROUP
    moment_ref[...] = jnp.zeros_like(moment_ref)
    first_ref[...] = jnp.zeros_like(first_ref)

    def taps_of(distance):
        out = jnp.zeros(distance.shape, F32)
        for k, tap in enumerate(TAPS):
            out = jnp.where(distance == k - 2, tap, out)
        return out

    source = lax.broadcasted_iota(jnp.int32, (2 * cols, 2 * cols), 0)
    target = lax.broadcasted_iota(jnp.int32, (2 * cols, 2 * cols), 1)
    band = jnp.where(
        source // cols == target // cols, taps_of(source % cols - target % cols), 0.0
    ).astype(BF16)
    source = lax.broadcasted_iota(jnp.int32, (128, 2 * cols), 0)
    target = lax.broadcasted_iota(jnp.int32, (128, 2 * cols), 1)
    is_low = source < 16
    pixel_row = (source % 16) // 2
    position = jnp.where(is_low, source % 2 - 2, cols + source % 2)
    sides = []
    for q in range(4):
        keep = (source < 32) & (pixel_row == 2 * q + target // cols)
        sides.append(jnp.where(keep, taps_of(position - target % cols), 0.0).astype(BF16))
    lane = lax.broadcasted_iota(jnp.int32, (bands, 128), 1)

    def side_lanes(chunk, shift):
        low = low_ref[:, 128 * chunk : 128 * chunk + 128].astype(F32)
        high = high_ref[:, 128 * chunk : 128 * chunk + 128].astype(F32)
        low = pltpu.roll(low, (128 - shift) % 128, 1)
        high = pltpu.roll(high, (128 + 16 - shift) % 128, 1)
        return jnp.where(lane < 16, low, jnp.where(lane < 32, high, 0.0)).astype(BF16)

    def smooth_pair(one, two, extra, q):
        pair = jnp.concatenate([one, two], axis=1)
        out = jnp.dot(pair, band, preferred_element_type=F32)
        out += jnp.dot(extra, sides[q], preferred_element_type=F32)
        return (out[:, :cols], out[:, cols:])

    def column_pass(g):
        if g < groups:
            extra = side_lanes(g // 8, 16 * (g % 8))
            for q in range(4):
                r = g * GROUP + 2 * q
                one, two = smooth_pair(xt_ref[r], xt_ref[r + 1], extra, q)
                col_ref[r + 2] = one
                col_ref[r + 3] = two
        elif g == groups:
            extra = side_lanes(groups // 8, 16 * (groups % 8))
            one, two = smooth_pair(down_ref[0], down_ref[1], extra, 1)
            col_ref[rows + 2] = one
            col_ref[rows + 3] = two

    def row_pass(g):
        base = g * GROUP
        weights = weight_ref[base : base + GROUP, :].astype(F32)
        field = [col_ref[base + i] for i in range(GROUP + 4)]
        parts = []
        total = None
        for i in range(GROUP):
            value = (
                0.0625 * (field[i] + field[i + 4])
                + 0.25 * (field[i + 1] + field[i + 3])
                + 0.375 * field[i + 2]
            )
            smooth_ref[base + i] = value
            value = value * weights[i : i + 1, :]
            total = value if total is None else total + value
            parts.append(value.astype(BF16))
        group_copy(smooth_ref, result_ref, sems, g).start()
        first_ref[...] += total
        flat = jnp.concatenate(parts, axis=1)
        moment_ref[...] += lax.dot_general(
            flat, flat, (((1,), (1,)), ((), ())), preferred_element_type=F32
        )

    extra = side_lanes(groups // 8, 16 * (groups % 8))
    one, two = smooth_pair(up_ref[0], up_ref[1], extra, 0)
    col_ref[0] = one
    col_ref[1] = two
    column_pass(0)
    column_pass(1)
    for g in range(groups):
        column_pass(g + 2)
        row_pass(g)

    put_folded(out_ref, moment_ref, first_ref, jnp.sum(weight_ref[...].astype(F32), keepdims=True))
    for g in range(groups):
        group_copy(smooth_ref, result_ref, sems, g).wait()


def signal_moments(xt, up, down, low, high, weight):
    rows, bands, cols = xt.shape
    return pl.pallas_call(
        signal_kernel,
        out_shape=(
            pltpu.HBM((rows, bands, cols), F32),
            jax.ShapeDtypeStruct((2, bands // 2, 128), F32),
        ),
        in_specs=[VMEM_SPEC] * 6,
        out_specs=(HBM_SPEC, VMEM_SPEC),
        scratch_shapes=[
            pltpu.VMEM((rows + 4, bands, cols), F32),
            pltpu.VMEM((bands, bands), F32),
            pltpu.VMEM((bands, cols), F32),
            pltpu.VMEM((rows, bands, cols), F32),
            pltpu.SemaphoreType.DMA((rows // GROUP,)),
        ],
        compiler_params=params(32),
        cost_estimate=cost(4 * bands * bands * rows * cols, 6 * bands * rows * cols),
        name="signal_moments",
    )(in_vmem(xt), up, down, low, high, weight)


def folded_of(sums_ref):
    return jnp.concatenate([sums_ref[0], sums_ref[1]], axis=1)


def sums_of(folded):
    size = 2 * folded.shape[0]
    first = jnp.concatenate(
        [folded[:, size + 2 : size + 3], folded[:, size + 3 : size + 4]], axis=0
    )
    return (first, folded[:1, size + 4 : size + 5])


def covariance_of(folded):
    size = 2 * folded.shape[0]
    first, count = sums_of(folded)
    down = jnp.broadcast_to(first, (size, 256))
    across = jnp.concatenate([down, jnp.zeros((256 - size, 256), F32)], axis=0).T[:size]
    return (unfold(folded) - down * across / count) / (count - 1.0)


def factor_into(work_ref, size):
    width = work_ref.shape[1]
    step = PIVOTS
    sub = lax.broadcasted_iota(jnp.int32, (step, 128), 0)
    lane = lax.broadcasted_iota(jnp.int32, (step, width), 1)
    sub_wide = lax.broadcasted_iota(jnp.int32, (step, width), 0)
    for base in range(0, size, step):
        low = base + step
        panel = work_ref[base:low, :]
        cols = [
            jnp.broadcast_to(panel[:, base + j : base + j + 1], (step, 128)) for j in range(step)
        ]
        eye = jnp.where(lane - base == sub_wide, 1.0, 0.0)
        rows = jnp.where((lane >= base) & (lane < low), eye, panel)
        scale = jnp.zeros((step, 128), F32)
        for j in range(step):
            root = lax.rsqrt(jnp.broadcast_to(cols[j][j : j + 1, :], (step, 128)))
            scale = jnp.where(sub == j, root, scale)
            if j < step - 1:
                ratio = jnp.where(sub > j, cols[j] * (root * root), 0.0)
                for i in range(j + 1, step):
                    cols[i] = cols[i] - ratio * jnp.broadcast_to(
                        cols[i][j : j + 1, :], (step, 128)
                    )
                ratio_wide = jnp.concatenate([ratio, ratio], axis=1)
                rows = rows - ratio_wide * jnp.broadcast_to(rows[j : j + 1, :], (step, width))
        rows = rows * jnp.concatenate([scale, scale], axis=1)
        work_ref[base:low, :] = jnp.where(lane < low, rows, 0.0)
        if low < size:
            cut = 128 if low >= 128 else 0
            one, two, three = split_three(rows)
            left = jnp.concatenate([one, one, two, two, one, three], axis=0)
            right = jnp.concatenate([one, two, one, two, three, one], axis=0)
            update = lax.dot_general(
                left[:, cut:], right, (((0,), (0,)), ((), ())), preferred_element_type=F32
            )
            rest = work_ref[low:size, :]
            rest_lane = lax.broadcasted_iota(jnp.int32, rest.shape, 1)
            rest = jnp.where((rest_lane >= base) & (rest_lane < low), 0.0, rest)
            work_ref[low:size, :] = rest - update[low - cut : size - cut, :]


def finish_kernel(
    noise_ref, signal_ref, weight_ref, field_ref, result_ref, cov_ref,
    work_ref, smooth_ref, out_ref, in_sems, out_sems,
):
    rows, bands, cols = smooth_ref.shape
    groups, slabs = rows // GROUP, rows // 16
    for g in range(groups):
        group_copy(field_ref, smooth_ref, in_sems, g).start()
    work_ref[...] = covariance_of(folded_of(noise_ref))
    factor_into(work_ref, bands)
    inverse = work_ref[:, :bands]
    inverse_cast = inverse.astype(BF16)
    first, count = sums_of(folded_of(signal_ref))
    mean = jnp.broadcast_to(first / count, (bands, cols))

    def outward(s):
        window = pl.ds(16 * s, 16)
        return pltpu.make_async_copy(out_ref.at[s], result_ref.at[:, window, :], out_sems.at[s])

    for s in range(slabs):
        base = 16 * s
        weights = weight_ref[base : base + 16, :].astype(F32)
        parts = []
        for pair in range(8):
            if pair % 4 == 0:
                group_copy(field_ref, smooth_ref, in_sems, 2 * s + pair // 4).wait()
            pieces = []
            for i in (2 * pair, 2 * pair + 1):
                pieces.append((weights[i : i + 1, :] * (smooth_ref[base + i] - mean)).astype(BF16))
            product = jnp.dot(
                inverse_cast, jnp.concatenate(pieces, axis=1), preferred_element_type=F32
            )
            product = product.astype(BF16)
            parts += [product[None, :, :cols], product[None, :, cols:]]
        out_ref[s] = jnp.swapaxes(jnp.concatenate(parts, axis=0), 0, 1)
        outward(s).start()

    cov = covariance_of(folded_of(signal_ref))[:, :bands]
    left = jnp.dot(inverse, cov, precision=lax.Precision.HIGHEST, preferred_element_type=F32)
    cov_ref[...] = lax.dot_general(
        left, inverse, (((1,), (1,)), ((), ())),
        precision=lax.Precision.HIGHEST, preferred_element_type=F32,
    )
    for s in range(slabs):
        outward(s).wait()


def finish(noise, signal, weight, smooth):
    rows, bands, cols = smooth.shape
    groups, slabs = rows // GROUP, rows // 16
    return pl.pallas_call(
        finish_kernel,
        out_shape=(
            pltpu.HBM((bands, rows, cols), BF16),
            jax.ShapeDtypeStruct((bands, bands), F32),
        ),
        in_specs=[VMEM_SPEC, VMEM_SPEC, VMEM_SPEC, HBM_SPEC],
        out_specs=(HBM_SPEC, VMEM_SPEC),
        scratch_shapes=[
            pltpu.VMEM((bands, 256), F32),
            pltpu.VMEM((rows, bands, cols), F32),
            pltpu.VMEM((slabs, bands, 16, cols), BF16),
            pltpu.SemaphoreType.DMA((groups,)),
            pltpu.SemaphoreType.DMA((slabs,)),
        ],
        compiler_params=params(36),
        cost_estimate=cost(2 * bands * bands * rows * cols, 6 * bands * rows * cols),
        name="finish",
    )(noise, signal, weight, in_hbm(smooth))


def line(count):
    forward = [(i, i + 1) for i in range(count - 1)]
    return (forward, [(target, source) for source, target in forward])


def body(radiance, valid_mask):
    first, last = edge_rows(radiance)
    forward, backward = line(lax.axis_size("tile"))
    up = lax.ppermute(last, "tile", forward)
    down = lax.ppermute(first, "tile", backward)
    xt, side, noise, noise_first = rows_first(radiance, valid_mask)
    to_low, to_high, noise = side_columns(
        side, up, down, first, last, valid_mask, noise, noise_first
    )
    forward, backward = line(lax.axis_size("group"))
    low = lax.ppermute(to_high, "group", forward)
    high = lax.ppermute(to_low, "group", backward)
    smooth, signal = signal_moments(xt, up, down, low, high, valid_mask)
    whitened, whitened_cov = finish(total_of(noise), total_of(signal), valid_mask, smooth)
    return (whitened, whitened_cov)


def solution(mesh):
    return jax.shard_map(
        body,
        mesh=mesh,
        in_specs=(P(None, "tile", "group"), P("tile", "group")),
        out_specs=(P(None, "tile", "group"), P()),
        check_vma=False,
    )
```

```python
import jax
import jax.numpy as jnp
from jax import lax
from jax.experimental import pallas as pl
from jax.experimental.pallas import tpu as pltpu
from jax.sharding import PartitionSpec as P

F32 = jnp.float32
BF16 = jnp.bfloat16
VMEM_SPEC = pl.BlockSpec(memory_space=pltpu.VMEM)
HBM_SPEC = pl.BlockSpec(memory_space=pltpu.HBM)
GROUP = 8
CORNER_GROUP = 12
PIVOTS = 16
TAPS = (0.0625, 0.25, 0.375, 0.25, 0.0625)


def flat_pairs(sizes, move):
    y_size, z_size, x_size = sizes
    pairs = []
    for y in range(y_size):
        for core in range(2):
            for z in range(z_size):
                for x in range(x_size):
                    y2, core2, z2, x2 = move(y, core, z, x)
                    source = ((y * 2 + core) * z_size + z) * x_size + x
                    target = ((y2 * 2 + core2) * z_size + z2) * x_size + x2
                    pairs.append((source, target))
    return pairs


SIZES = (4, 8, 4)
CORE_SWAP = flat_pairs(SIZES, lambda y, c, z, x: (y, 1 - c, z, x))
STAGES = (
    [flat_pairs(SIZES, lambda y, c, z, x, k=k: (y, c, z, x ^ k)) for k in (1, 2, 3)],
    [flat_pairs(SIZES, lambda y, c, z, x, k=k: (y ^ k, c, z, x)) for k in (1, 2, 3)],
    [flat_pairs(SIZES, lambda y, c, z, x, k=k: (y, c, z ^ k, x)) for k in (1, 2, 3)],
    [flat_pairs(SIZES, lambda y, c, z, x: (y, c, 7 - z, x))],
)
AXES = ("group", "tile")


def total_of(value, beside=None):
    first = lax.axis_index("group") % 2 == 0
    own = jnp.where(first, value[0], value[1])
    other = jnp.where(first, value[1], value[0])
    own = own + lax.ppermute(other, AXES, CORE_SWAP)
    for stage in STAGES:
        parts = [lax.ppermute(own, AXES, pairs) for pairs in stage]
        if len(parts) == 1:
            part = parts[0]
            if beside is not None:
                part, beside = lax.optimization_barrier((part, beside))
            own = own + part
        else:
            own = (own + parts[0]) + (parts[1] + parts[2])
    other = lax.ppermute(own, AXES, CORE_SWAP)
    return (jnp.stack([jnp.where(first, own, other), jnp.where(first, other, own)]), beside)


def split_three(value):
    first = value.astype(jnp.bfloat16)
    rest = value - first.astype(jnp.float32)
    second = rest.astype(jnp.bfloat16)
    third = (rest - second.astype(jnp.float32)).astype(jnp.bfloat16)
    return (first, second, third)


def params(mebibytes):
    return pltpu.CompilerParams(vmem_limit_bytes=mebibytes << 20)


def cost(flops, bytes_accessed):
    return pl.CostEstimate(flops=flops, bytes_accessed=bytes_accessed, transcendentals=0)


def in_hbm(value):
    return pltpu.with_memory_space_constraint(value, pltpu.HBM)


def in_vmem(value):
    return pltpu.with_memory_space_constraint(value, pltpu.VMEM)


def edges_kernel(x_ref, first_ref, last_ref, slab_ref, sems):
    rows = x_ref.shape[1]
    top = pltpu.make_async_copy(x_ref.at[:, pl.ds(0, 16), :], slab_ref.at[0], sems.at[0])
    low = pltpu.make_async_copy(x_ref.at[:, pl.ds(rows - 16, 16), :], slab_ref.at[1], sems.at[1])
    top.start()
    low.start()
    top.wait()
    first_ref[...] = jnp.swapaxes(slab_ref[0], 0, 1)[:2]
    low.wait()
    last_ref[...] = jnp.swapaxes(slab_ref[1], 0, 1)[14:]


def edge_rows(x):
    bands, rows, cols = x.shape
    shape = jax.ShapeDtypeStruct((2, bands, cols), BF16)
    return pl.pallas_call(
        edges_kernel,
        out_shape=(shape, shape),
        in_specs=[HBM_SPEC],
        out_specs=(VMEM_SPEC, VMEM_SPEC),
        scratch_shapes=[pltpu.VMEM((2, bands, 16, cols), BF16), pltpu.SemaphoreType.DMA((2,))],
        compiler_params=params(8),
        cost_estimate=cost(0, 4 * bands * 16 * cols),
        name="edge_rows",
    )(in_hbm(x))


def side_picker(cols):
    place = lax.broadcasted_iota(jnp.int32, (GROUP * cols, 128), 0)
    lane = lax.broadcasted_iota(jnp.int32, (GROUP * cols, 128), 1)
    pixel_row, col = place // cols, place % cols
    wanted_low = 2 * pixel_row + col
    wanted_high = 2 * GROUP + 2 * pixel_row + (col - (cols - 2))
    pick = ((col < 2) & (lane == wanted_low)) | ((col >= cols - 2) & (lane == wanted_high))
    return jnp.where(pick, 1.0, 0.0).astype(BF16)


def side_lanes_of(pieces, pick, g):
    got = jnp.dot(jnp.concatenate(pieces, axis=1), pick, preferred_element_type=F32)
    lane = lax.broadcasted_iota(jnp.int32, got.shape, 1)
    shift = 16 * (g % 8)
    turn = (shift - 16) % 128
    low = jnp.where(lane < 16, got, 0.0)
    high = jnp.where((lane >= 16) & (lane < 32), got, 0.0)
    return (
        pltpu.roll(low, shift, 1) if shift else low,
        pltpu.roll(high, turn, 1) if turn else high,
    )


def noise_rows(row_of, weight_ref, rows, moment_ref, first_ref):
    parts = []
    total = None
    for r in rows:
        value = row_of(r) - 0.5 * (row_of(r - 1) + row_of(r + 1))
        value = value * weight_ref[r : r + 1, :].astype(F32)
        total = value if total is None else total + value
        parts.append(value.astype(BF16))
    first_ref[...] += total
    flat = jnp.concatenate(parts, axis=1)
    moment_ref[...] += lax.dot_general(
        flat, flat, (((1,), (1,)), ((), ())), preferred_element_type=F32
    )


def rows_first_kernel(
    x_ref, weight_ref, out_ref, side_ref, moment_ref, first_ref,
    slab_ref, turned_ref, in_sems, out_sems,
):
    slabs, bands, _, cols = slab_ref.shape
    rows = 16 * slabs

    def row_of(r):
        return turned_ref[r].astype(F32)

    inward = [
        pltpu.make_async_copy(x_ref.at[:, pl.ds(16 * s, 16), :], slab_ref.at[s], in_sems.at[s])
        for s in range(slabs)
    ]
    due = {begin: range(begin, end) for begin, end in spans_of(slabs)}
    outward = [
        pltpu.make_async_copy(
            turned_ref.at[pl.ds(16 * s, 16)], out_ref.at[pl.ds(16 * s, 16)], out_sems.at[s]
        )
        for s in range(slabs)
    ]
    for copy in inward:
        copy.start()
    moment_ref[...] = jnp.zeros_like(moment_ref)
    first_ref[...] = jnp.zeros_like(first_ref)
    pick = side_picker(cols)
    sums = [[jnp.zeros((bands, 128), F32) for _ in range(2)] for _ in range(2)]
    for s in range(slabs):
        for later in due.get(s, ()):
            inward[later].wait()
        turned_ref[16 * s : 16 * s + 16] = jnp.swapaxes(slab_ref[s], 0, 1)
        outward[s].start()
        for g in (2 * s, 2 * s + 1):
            pieces = [turned_ref[g * GROUP + i] for i in range(GROUP)]
            low, high = side_lanes_of(pieces, pick, g)
            sums[0][g // 8] += low
            sums[1][g // 8] += high
        start = max(16 * s - 7, 1)
        for base in range(start, 16 * s + 15, 8):
            stop = min(base + 8, 16 * s + 9 if s < slabs - 1 else rows - 1)
            if base < stop:
                noise_rows(row_of, weight_ref, range(base, stop), moment_ref, first_ref)
    for side in range(2):
        side_ref[side] = jnp.concatenate(sums[side], axis=1).astype(BF16)
    for copy in outward:
        copy.wait()


def rows_first(x, weight):
    bands, rows, cols = x.shape
    slabs = rows // 16
    return pl.pallas_call(
        rows_first_kernel,
        out_shape=(
            pltpu.HBM((rows, bands, cols), BF16),
            jax.ShapeDtypeStruct((2, bands, 256), BF16),
            jax.ShapeDtypeStruct((bands, bands), F32),
            jax.ShapeDtypeStruct((bands, cols), F32),
        ),
        in_specs=[HBM_SPEC, VMEM_SPEC],
        out_specs=(HBM_SPEC, VMEM_SPEC, VMEM_SPEC, VMEM_SPEC),
        scratch_shapes=[
            pltpu.VMEM((slabs, bands, 16, cols), BF16),
            pltpu.VMEM((rows, bands, cols), BF16),
            pltpu.SemaphoreType.DMA((slabs,)),
            pltpu.SemaphoreType.DMA((slabs,)),
        ],
        compiler_params=params(20),
        cost_estimate=cost(2 * bands * bands * rows * cols, 4 * bands * rows * cols),
        name="rows_first",
    )(in_hbm(x), weight)


def put_folded(out_ref, moment_ref, first_ref, count):
    half = moment_ref.shape[0] // 2
    first = jnp.sum(first_ref[...], axis=1, keepdims=True)
    folded = fold(moment_ref[...], [first[:half], first[half:], count])
    out_ref[0] = folded[:, :128]
    out_ref[1] = folded[:, 128:]


def corners_kernel(
    side_ref, up_ref, down_ref, top_ref, bottom_ref, weight_ref, noise_ref, noise_first_ref,
    low_ref, high_ref, out_ref, moment_ref, first_ref,
):
    bands, cols = up_ref.shape[1:]
    rows = weight_ref.shape[0]
    zero = jnp.zeros((bands, cols), BF16)
    pieces = [up_ref[0], up_ref[1], down_ref[0], down_ref[1]] + [zero] * 4
    parts = side_lanes_of(pieces, side_picker(cols), CORNER_GROUP)
    for side, side_out_ref in ((0, low_ref), (1, high_ref)):
        side_out_ref[:, :128] = side_ref[side][:, :128]
        side_out_ref[:, 128:] = (side_ref[side][:, 128:].astype(F32) + parts[side]).astype(BF16)

    def row_of(r):
        if r < 2:
            row = up_ref[1] if r < 0 else top_ref[r]
        else:
            row = down_ref[0] if r == rows else bottom_ref[r - rows + 2]
        return row.astype(F32)

    moment_ref[...] = noise_ref[...]
    first_ref[...] = noise_first_ref[...]
    noise_rows(row_of, weight_ref, (0, rows - 1), moment_ref, first_ref)
    count = jnp.sum(weight_ref[...].astype(F32), keepdims=True)
    put_folded(out_ref, moment_ref, first_ref, count)


def side_columns(side, up, down, top, bottom, weight, noise, noise_first):
    bands = side.shape[1]
    shape = jax.ShapeDtypeStruct((bands, 256), BF16)
    return pl.pallas_call(
        corners_kernel,
        out_shape=(shape, shape, jax.ShapeDtypeStruct((2, bands // 2, 128), F32)),
        in_specs=[VMEM_SPEC] * 8,
        out_specs=(VMEM_SPEC,) * 3,
        scratch_shapes=[pltpu.VMEM((bands, bands), F32), pltpu.VMEM(noise_first.shape, F32)],
        compiler_params=params(10),
        cost_estimate=cost(2 * bands * 1024 * 128, 6 * bands * 256),
        name="side_columns",
    )(side, up, down, top, bottom, weight, noise, noise_first)


def spans_of(count):
    marks = (0, count // 6, count // 2, count)
    return list(zip(marks[:-1], marks[1:]))


def group_copy(source_ref, target_ref, sems, g):
    start = g * GROUP if isinstance(g, int) else pl.multiple_of(g * GROUP, GROUP)
    window = pl.ds(start, GROUP)
    return pltpu.make_async_copy(source_ref.at[window], target_ref.at[window], sems.at[g])


def fold(moment, columns):
    size = moment.shape[0]
    half = size // 2
    wide = moment if moment.shape[1] == 256 else jnp.concatenate(
        [moment, jnp.zeros((size, 256 - size), F32)], axis=1
    )
    row = lax.broadcasted_iota(jnp.int32, (half, 256), 0)
    lane = lax.broadcasted_iota(jnp.int32, (half, 256), 1)
    moved = pltpu.roll(wide[:half], half + 1, 1)
    out = jnp.where(lane <= half + row, wide[half:], moved)
    for place, column in enumerate(columns):
        out = jnp.where(lane == size + 2 + place, column, out)
    return out


def unfold(folded):
    half = folded.shape[0]
    size = 2 * half
    row = lax.broadcasted_iota(jnp.int32, (half, 256), 0)
    lane = lax.broadcasted_iota(jnp.int32, (half, 256), 1)
    back = pltpu.roll(folded, 256 - half - 1, 1)
    upper = jnp.where((lane >= row) & (lane < half), back, 0.0)
    lower = jnp.where(lane <= half + row, folded, 0.0)
    part = jnp.concatenate([upper, lower], axis=0)
    turned = jnp.concatenate([part, jnp.zeros((256 - size, 256), F32)], axis=0).T[:size]
    row = lax.broadcasted_iota(jnp.int32, (size, 256), 0)
    lane = lax.broadcasted_iota(jnp.int32, (size, 256), 1)
    return part + jnp.where(row == lane, 0.0, turned)


def signal_kernel(
    xt_ref, up_ref, down_ref, low_ref, high_ref, weight_ref,
    result_ref, out_ref, col_ref, moment_ref, first_ref, smooth_ref, sems,
):
    rows, bands, cols = xt_ref.shape
    groups = rows // GROUP
    moment_ref[...] = jnp.zeros_like(moment_ref)
    first_ref[...] = jnp.zeros_like(first_ref)

    def taps_of(distance):
        out = jnp.zeros(distance.shape, F32)
        for k, tap in enumerate(TAPS):
            out = jnp.where(distance == k - 2, tap, out)
        return out

    source = lax.broadcasted_iota(jnp.int32, (2 * cols, 2 * cols), 0)
    target = lax.broadcasted_iota(jnp.int32, (2 * cols, 2 * cols), 1)
    band = jnp.where(
        source // cols == target // cols, taps_of(source % cols - target % cols), 0.0
    ).astype(BF16)
    source = lax.broadcasted_iota(jnp.int32, (128, 2 * cols), 0)
    target = lax.broadcasted_iota(jnp.int32, (128, 2 * cols), 1)
    is_low = source < 16
    pixel_row = (source % 16) // 2
    position = jnp.where(is_low, source % 2 - 2, cols + source % 2)
    sides = []
    for q in range(4):
        keep = (source < 32) & (pixel_row == 2 * q + target // cols)
        sides.append(jnp.where(keep, taps_of(position - target % cols), 0.0).astype(BF16))
    lane = lax.broadcasted_iota(jnp.int32, (bands, 128), 1)

    def side_lanes(chunk, shift):
        low = low_ref[:, 128 * chunk : 128 * chunk + 128].astype(F32)
        high = high_ref[:, 128 * chunk : 128 * chunk + 128].astype(F32)
        low = pltpu.roll(low, (128 - shift) % 128, 1)
        high = pltpu.roll(high, (128 + 16 - shift) % 128, 1)
        return jnp.where(lane < 16, low, jnp.where(lane < 32, high, 0.0)).astype(BF16)

    def smooth_pair(one, two, extra, q):
        pair = jnp.concatenate([one, two], axis=1)
        out = jnp.dot(pair, band, preferred_element_type=F32)
        out += jnp.dot(extra, sides[q], preferred_element_type=F32)
        return (out[:, :cols], out[:, cols:])

    def column_pass(g):
        if g < groups:
            extra = side_lanes(g // 8, 16 * (g % 8))
            for q in range(4):
                r = g * GROUP + 2 * q
                one, two = smooth_pair(xt_ref[r], xt_ref[r + 1], extra, q)
                col_ref[r + 2] = one
                col_ref[r + 3] = two
        elif g == groups:
            extra = side_lanes(groups // 8, 16 * (groups % 8))
            one, two = smooth_pair(down_ref[0], down_ref[1], extra, 1)
            col_ref[rows + 2] = one
            col_ref[rows + 3] = two

    def row_pass(g):
        base = g * GROUP
        weights = weight_ref[base : base + GROUP, :].astype(F32)
        field = [col_ref[base + i] for i in range(GROUP + 4)]
        parts = []
        total = None
        for i in range(GROUP):
            value = (
                0.0625 * (field[i] + field[i + 4])
                + 0.25 * (field[i + 1] + field[i + 3])
                + 0.375 * field[i + 2]
            )
            smooth_ref[base + i] = value
            value = value * weights[i : i + 1, :]
            total = value if total is None else total + value
            parts.append(value.astype(BF16))
        group_copy(smooth_ref, result_ref, sems, g).start()
        first_ref[...] += total
        flat = jnp.concatenate(parts, axis=1)
        moment_ref[...] += lax.dot_general(
            flat, flat, (((1,), (1,)), ((), ())), preferred_element_type=F32
        )

    extra = side_lanes(groups // 8, 16 * (groups % 8))
    one, two = smooth_pair(up_ref[0], up_ref[1], extra, 0)
    col_ref[0] = one
    col_ref[1] = two
    column_pass(0)
    column_pass(1)
    for g in range(groups):
        column_pass(g + 2)
        row_pass(g)

    put_folded(out_ref, moment_ref, first_ref, jnp.sum(weight_ref[...].astype(F32), keepdims=True))
    for g in range(groups):
        group_copy(smooth_ref, result_ref, sems, g).wait()


def signal_moments(xt, up, down, low, high, weight):
    rows, bands, cols = xt.shape
    return pl.pallas_call(
        signal_kernel,
        out_shape=(
            pltpu.HBM((rows, bands, cols), F32),
            jax.ShapeDtypeStruct((2, bands // 2, 128), F32),
        ),
        in_specs=[VMEM_SPEC] * 6,
        out_specs=(HBM_SPEC, VMEM_SPEC),
        scratch_shapes=[
            pltpu.VMEM((rows + 4, bands, cols), F32),
            pltpu.VMEM((bands, bands), F32),
            pltpu.VMEM((bands, cols), F32),
            pltpu.VMEM((rows, bands, cols), F32),
            pltpu.SemaphoreType.DMA((rows // GROUP,)),
        ],
        compiler_params=params(32),
        cost_estimate=cost(4 * bands * bands * rows * cols, 6 * bands * rows * cols),
        name="signal_moments",
    )(in_vmem(xt), up, down, low, high, weight)


def folded_of(sums_ref):
    return jnp.concatenate([sums_ref[0], sums_ref[1]], axis=1)


def sums_of(folded):
    size = 2 * folded.shape[0]
    first = jnp.concatenate(
        [folded[:, size + 2 : size + 3], folded[:, size + 3 : size + 4]], axis=0
    )
    return (first, folded[:1, size + 4 : size + 5])


def covariance_of(folded):
    size = 2 * folded.shape[0]
    first, count = sums_of(folded)
    down = jnp.broadcast_to(first, (size, 256))
    across = jnp.concatenate([down, jnp.zeros((256 - size, 256), F32)], axis=0).T[:size]
    return (unfold(folded) - down * across / count) / (count - 1.0)


def factor_into(work_ref, size):
    width = work_ref.shape[1]
    step = PIVOTS
    sub = lax.broadcasted_iota(jnp.int32, (step, 128), 0)
    lane = lax.broadcasted_iota(jnp.int32, (step, width), 1)
    sub_wide = lax.broadcasted_iota(jnp.int32, (step, width), 0)
    for base in range(0, size, step):
        low = base + step
        panel = work_ref[base:low, :]
        cols = [
            jnp.broadcast_to(panel[:, base + j : base + j + 1], (step, 128)) for j in range(step)
        ]
        eye = jnp.where(lane - base == sub_wide, 1.0, 0.0)
        rows = jnp.where((lane >= base) & (lane < low), eye, panel)
        scale = jnp.zeros((step, 128), F32)
        for j in range(step):
            root = lax.rsqrt(jnp.broadcast_to(cols[j][j : j + 1, :], (step, 128)))
            scale = jnp.where(sub == j, root, scale)
            if j < step - 1:
                ratio = jnp.where(sub > j, cols[j] * (root * root), 0.0)
                for i in range(j + 1, step):
                    cols[i] = cols[i] - ratio * jnp.broadcast_to(
                        cols[i][j : j + 1, :], (step, 128)
                    )
                ratio_wide = jnp.concatenate([ratio, ratio], axis=1)
                rows = rows - ratio_wide * jnp.broadcast_to(rows[j : j + 1, :], (step, width))
        rows = rows * jnp.concatenate([scale, scale], axis=1)
        work_ref[base:low, :] = jnp.where(lane < low, rows, 0.0)
        if low < size:
            cut = 128 if low >= 128 else 0
            one, two, three = split_three(rows)
            left = jnp.concatenate([one, one, two, two, one, three], axis=0)
            right = jnp.concatenate([one, two, one, two, three, one], axis=0)
            update = lax.dot_general(
                left[:, cut:], right, (((0,), (0,)), ((), ())), preferred_element_type=F32
            )
            rest = work_ref[low:size, :]
            rest_lane = lax.broadcasted_iota(jnp.int32, rest.shape, 1)
            rest = jnp.where((rest_lane >= base) & (rest_lane < low), 0.0, rest)
            work_ref[low:size, :] = rest - update[low - cut : size - cut, :]


def factor_kernel(noise_ref, out_ref, work_ref):
    size = out_ref.shape[0]
    work_ref[...] = covariance_of(folded_of(noise_ref))
    factor_into(work_ref, size)
    out_ref[...] = work_ref[:, :size]


def inverse_factor(noise):
    size = 2 * noise.shape[1]
    return pl.pallas_call(
        factor_kernel,
        out_shape=jax.ShapeDtypeStruct((size, size), F32),
        in_specs=[VMEM_SPEC],
        out_specs=VMEM_SPEC,
        scratch_shapes=[pltpu.VMEM((size, 256), F32)],
        compiler_params=params(6),
        cost_estimate=cost(400 * size**3, 8 * size**2),
        name="inverse_factor",
    )(noise)


def finish_kernel(
    inverse_ref, signal_ref, weight_ref, field_ref, result_ref, cov_ref,
    smooth_ref, out_ref, in_sems, out_sems,
):
    rows, bands, cols = smooth_ref.shape
    groups, slabs = rows // GROUP, rows // 16
    for g in range(groups):
        group_copy(field_ref, smooth_ref, in_sems, g).start()
    inverse = inverse_ref[...]
    cov = covariance_of(folded_of(signal_ref))[:, :bands]
    left = jnp.dot(inverse, cov, precision=lax.Precision.HIGHEST, preferred_element_type=F32)
    cov_ref[...] = lax.dot_general(
        left, inverse, (((1,), (1,)), ((), ())),
        precision=lax.Precision.HIGHEST, preferred_element_type=F32,
    )
    inverse_cast = inverse.astype(BF16)
    first, count = sums_of(folded_of(signal_ref))
    mean = jnp.broadcast_to(first / count, (bands, cols))

    def outward(s):
        window = pl.ds(16 * s, 16)
        return pltpu.make_async_copy(out_ref.at[s], result_ref.at[:, window, :], out_sems.at[s])

    for s in range(slabs):
        base = 16 * s
        weights = weight_ref[base : base + 16, :].astype(F32)
        parts = []
        for pair in range(8):
            if pair % 4 == 0:
                group_copy(field_ref, smooth_ref, in_sems, 2 * s + pair // 4).wait()
            pieces = []
            for i in (2 * pair, 2 * pair + 1):
                pieces.append((weights[i : i + 1, :] * (smooth_ref[base + i] - mean)).astype(BF16))
            product = jnp.dot(
                inverse_cast, jnp.concatenate(pieces, axis=1), preferred_element_type=F32
            )
            product = product.astype(BF16)
            parts += [product[None, :, :cols], product[None, :, cols:]]
        out_ref[s] = jnp.swapaxes(jnp.concatenate(parts, axis=0), 0, 1)
        outward(s).start()

    for s in range(slabs):
        outward(s).wait()


def finish(inverse, signal, weight, smooth):
    rows, bands, cols = smooth.shape
    groups, slabs = rows // GROUP, rows // 16
    return pl.pallas_call(
        finish_kernel,
        out_shape=(
            pltpu.HBM((bands, rows, cols), BF16),
            jax.ShapeDtypeStruct((bands, bands), F32),
        ),
        in_specs=[VMEM_SPEC, VMEM_SPEC, VMEM_SPEC, HBM_SPEC],
        out_specs=(HBM_SPEC, VMEM_SPEC),
        scratch_shapes=[
            pltpu.VMEM((rows, bands, cols), F32),
            pltpu.VMEM((slabs, bands, 16, cols), BF16),
            pltpu.SemaphoreType.DMA((groups,)),
            pltpu.SemaphoreType.DMA((slabs,)),
        ],
        compiler_params=params(36),
        cost_estimate=cost(2 * bands * bands * rows * cols, 6 * bands * rows * cols),
        name="finish",
    )(inverse, signal, weight, in_hbm(smooth))


def line(count):
    forward = [(i, i + 1) for i in range(count - 1)]
    return (forward, [(target, source) for source, target in forward])


def body(radiance, valid_mask):
    first, last = edge_rows(radiance)
    forward, backward = line(lax.axis_size("tile"))
    up = lax.ppermute(last, "tile", forward)
    down = lax.ppermute(first, "tile", backward)
    xt, side, noise, noise_first = rows_first(radiance, valid_mask)
    to_low, to_high, noise = side_columns(
        side, up, down, first, last, valid_mask, noise, noise_first
    )
    forward, backward = line(lax.axis_size("group"))
    low = lax.ppermute(to_high, "group", forward)
    high = lax.ppermute(to_low, "group", backward)
    smooth, signal = signal_moments(xt, up, down, low, high, valid_mask)
    noise_total, _ = total_of(noise)
    signal_total, inverse = total_of(signal, inverse_factor(noise_total))
    whitened, whitened_cov = finish(inverse, signal_total, valid_mask, smooth)
    return (whitened, whitened_cov)


def solution(mesh):
    return jax.shard_map(
        body,
        mesh=mesh,
        in_specs=(P(None, "tile", "group"), P("tile", "group")),
        out_specs=(P(None, "tile", "group"), P()),
        check_vma=False,
    )
```

```python
import jax
import jax.numpy as jnp
from jax import lax
from jax.experimental import pallas as pl
from jax.experimental.pallas import tpu as pltpu
from jax.sharding import PartitionSpec as P

F32 = jnp.float32
BF16 = jnp.bfloat16
VMEM_SPEC = pl.BlockSpec(memory_space=pltpu.VMEM)
HBM_SPEC = pl.BlockSpec(memory_space=pltpu.HBM)
GROUP = 8
CORNER_GROUP = 12
PIVOTS = 16
TAPS = (0.0625, 0.25, 0.375, 0.25, 0.0625)


def flat_pairs(sizes, move):
    y_size, z_size, x_size = sizes
    pairs = []
    for y in range(y_size):
        for core in range(2):
            for z in range(z_size):
                for x in range(x_size):
                    y2, core2, z2, x2 = move(y, core, z, x)
                    source = ((y * 2 + core) * z_size + z) * x_size + x
                    target = ((y2 * 2 + core2) * z_size + z2) * x_size + x2
                    pairs.append((source, target))
    return pairs


SIZES = (4, 8, 4)
CORE_SWAP = flat_pairs(SIZES, lambda y, c, z, x: (y, 1 - c, z, x))
STAGES = (
    [flat_pairs(SIZES, lambda y, c, z, x, k=k: (y, c, z, x ^ k)) for k in (1, 2, 3)],
    [flat_pairs(SIZES, lambda y, c, z, x, k=k: (y ^ k, c, z, x)) for k in (1, 2, 3)],
    [flat_pairs(SIZES, lambda y, c, z, x, k=k: (y, c, z ^ k, x)) for k in (1, 2, 3)],
    [flat_pairs(SIZES, lambda y, c, z, x: (y, c, 7 - z, x))],
)
AXES = ("group", "tile")


def total_of(value, beside=None):
    first = lax.axis_index("group") % 2 == 0
    own = jnp.where(first, value[0], value[1])
    other = jnp.where(first, value[1], value[0])
    own = own + lax.ppermute(other, AXES, CORE_SWAP)
    for stage in STAGES:
        parts = [lax.ppermute(own, AXES, pairs) for pairs in stage]
        if len(parts) == 1:
            part = parts[0]
            if beside is not None:
                part, beside = lax.optimization_barrier((part, beside))
            own = own + part
        else:
            own = (own + parts[0]) + (parts[1] + parts[2])
    other = lax.ppermute(own, AXES, CORE_SWAP)
    return (jnp.stack([jnp.where(first, own, other), jnp.where(first, other, own)]), beside)


def split_three(value):
    first = value.astype(jnp.bfloat16)
    rest = value - first.astype(jnp.float32)
    second = rest.astype(jnp.bfloat16)
    third = (rest - second.astype(jnp.float32)).astype(jnp.bfloat16)
    return (first, second, third)


def params(mebibytes):
    return pltpu.CompilerParams(vmem_limit_bytes=mebibytes << 20)


def cost(flops, bytes_accessed):
    return pl.CostEstimate(flops=flops, bytes_accessed=bytes_accessed, transcendentals=0)


def in_hbm(value):
    return pltpu.with_memory_space_constraint(value, pltpu.HBM)


def in_vmem(value):
    return pltpu.with_memory_space_constraint(value, pltpu.VMEM)


def edges_kernel(x_ref, first_ref, last_ref, slab_ref, sems):
    rows = x_ref.shape[1]
    top = pltpu.make_async_copy(x_ref.at[:, pl.ds(0, 16), :], slab_ref.at[0], sems.at[0])
    low = pltpu.make_async_copy(x_ref.at[:, pl.ds(rows - 16, 16), :], slab_ref.at[1], sems.at[1])
    top.start()
    low.start()
    top.wait()
    first_ref[...] = jnp.swapaxes(slab_ref[0], 0, 1)[:2]
    low.wait()
    last_ref[...] = jnp.swapaxes(slab_ref[1], 0, 1)[14:]


def edge_rows(x):
    bands, rows, cols = x.shape
    shape = jax.ShapeDtypeStruct((2, bands, cols), BF16)
    return pl.pallas_call(
        edges_kernel,
        out_shape=(shape, shape),
        in_specs=[HBM_SPEC],
        out_specs=(VMEM_SPEC, VMEM_SPEC),
        scratch_shapes=[pltpu.VMEM((2, bands, 16, cols), BF16), pltpu.SemaphoreType.DMA((2,))],
        compiler_params=params(8),
        cost_estimate=cost(0, 4 * bands * 16 * cols),
        name="edge_rows",
    )(in_hbm(x))


def side_picker(cols):
    place = lax.broadcasted_iota(jnp.int32, (GROUP * cols, 128), 0)
    lane = lax.broadcasted_iota(jnp.int32, (GROUP * cols, 128), 1)
    pixel_row, col = place // cols, place % cols
    wanted_low = 2 * pixel_row + col
    wanted_high = 2 * GROUP + 2 * pixel_row + (col - (cols - 2))
    pick = ((col < 2) & (lane == wanted_low)) | ((col >= cols - 2) & (lane == wanted_high))
    return jnp.where(pick, 1.0, 0.0).astype(BF16)


def side_lanes_of(pieces, pick, g):
    got = jnp.dot(jnp.concatenate(pieces, axis=1), pick, preferred_element_type=F32)
    lane = lax.broadcasted_iota(jnp.int32, got.shape, 1)
    shift = 16 * (g % 8)
    turn = (shift - 16) % 128
    low = jnp.where(lane < 16, got, 0.0)
    high = jnp.where((lane >= 16) & (lane < 32), got, 0.0)
    return (
        pltpu.roll(low, shift, 1) if shift else low,
        pltpu.roll(high, turn, 1) if turn else high,
    )


def noise_rows(row_of, weight_ref, rows, moment_ref, first_ref):
    parts = []
    total = None
    for r in rows:
        value = row_of(r) - 0.5 * (row_of(r - 1) + row_of(r + 1))
        value = value * weight_ref[r : r + 1, :].astype(F32)
        total = value if total is None else total + value
        parts.append(value.astype(BF16))
    first_ref[...] += total
    flat = jnp.concatenate(parts, axis=1)
    moment_ref[...] += lax.dot_general(
        flat, flat, (((1,), (1,)), ((), ())), preferred_element_type=F32
    )


def rows_first_kernel(
    x_ref, weight_ref, out_ref, side_ref, moment_ref, first_ref,
    slab_ref, turned_ref, in_sems, out_sems,
):
    slabs, bands, _, cols = slab_ref.shape
    rows = 16 * slabs

    def row_of(r):
        return turned_ref[r].astype(F32)

    inward = [
        pltpu.make_async_copy(x_ref.at[:, pl.ds(16 * s, 16), :], slab_ref.at[s], in_sems.at[s])
        for s in range(slabs)
    ]
    due = {begin: range(begin, end) for begin, end in spans_of(slabs)}
    outward = [
        pltpu.make_async_copy(
            turned_ref.at[pl.ds(16 * s, 16)], out_ref.at[pl.ds(16 * s, 16)], out_sems.at[s]
        )
        for s in range(slabs)
    ]
    for copy in inward:
        copy.start()
    moment_ref[...] = jnp.zeros_like(moment_ref)
    first_ref[...] = jnp.zeros_like(first_ref)
    pick = side_picker(cols)
    sums = [[jnp.zeros((bands, 128), F32) for _ in range(2)] for _ in range(2)]
    for s in range(slabs):
        for later in due.get(s, ()):
            inward[later].wait()
        turned_ref[16 * s : 16 * s + 16] = jnp.swapaxes(slab_ref[s], 0, 1)
        outward[s].start()
        for g in (2 * s, 2 * s + 1):
            pieces = [turned_ref[g * GROUP + i] for i in range(GROUP)]
            low, high = side_lanes_of(pieces, pick, g)
            sums[0][g // 8] += low
            sums[1][g // 8] += high
        start = max(16 * s - 7, 1)
        for base in range(start, 16 * s + 15, 8):
            stop = min(base + 8, 16 * s + 9 if s < slabs - 1 else rows - 1)
            if base < stop:
                noise_rows(row_of, weight_ref, range(base, stop), moment_ref, first_ref)
    for side in range(2):
        side_ref[side] = jnp.concatenate(sums[side], axis=1).astype(BF16)
    for copy in outward:
        copy.wait()


def rows_first(x, weight):
    bands, rows, cols = x.shape
    slabs = rows // 16
    return pl.pallas_call(
        rows_first_kernel,
        out_shape=(
            pltpu.HBM((rows, bands, cols), BF16),
            jax.ShapeDtypeStruct((2, bands, 256), BF16),
            jax.ShapeDtypeStruct((bands, bands), F32),
            jax.ShapeDtypeStruct((bands, cols), F32),
        ),
        in_specs=[HBM_SPEC, VMEM_SPEC],
        out_specs=(HBM_SPEC, VMEM_SPEC, VMEM_SPEC, VMEM_SPEC),
        scratch_shapes=[
            pltpu.VMEM((slabs, bands, 16, cols), BF16),
            pltpu.VMEM((rows, bands, cols), BF16),
            pltpu.SemaphoreType.DMA((slabs,)),
            pltpu.SemaphoreType.DMA((slabs,)),
        ],
        compiler_params=params(20),
        cost_estimate=cost(2 * bands * bands * rows * cols, 4 * bands * rows * cols),
        name="rows_first",
    )(in_hbm(x), weight)


def put_folded(out_ref, moment_ref, first_ref, count):
    half = moment_ref.shape[0] // 2
    first = jnp.sum(first_ref[...], axis=1, keepdims=True)
    folded = fold(moment_ref[...], [first[:half], first[half:], count])
    out_ref[0] = folded[:, :128]
    out_ref[1] = folded[:, 128:]


def corners_kernel(
    side_ref, up_ref, down_ref, top_ref, bottom_ref, weight_ref, noise_ref, noise_first_ref,
    low_ref, high_ref, out_ref, moment_ref, first_ref,
):
    bands, cols = up_ref.shape[1:]
    rows = weight_ref.shape[0]
    zero = jnp.zeros((bands, cols), BF16)
    pieces = [up_ref[0], up_ref[1], down_ref[0], down_ref[1]] + [zero] * 4
    parts = side_lanes_of(pieces, side_picker(cols), CORNER_GROUP)
    for side, side_out_ref in ((0, low_ref), (1, high_ref)):
        side_out_ref[:, :128] = side_ref[side][:, :128]
        side_out_ref[:, 128:] = (side_ref[side][:, 128:].astype(F32) + parts[side]).astype(BF16)

    def row_of(r):
        if r < 2:
            row = up_ref[1] if r < 0 else top_ref[r]
        else:
            row = down_ref[0] if r == rows else bottom_ref[r - rows + 2]
        return row.astype(F32)

    moment_ref[...] = noise_ref[...]
    first_ref[...] = noise_first_ref[...]
    noise_rows(row_of, weight_ref, (0, rows - 1), moment_ref, first_ref)
    count = jnp.sum(weight_ref[...].astype(F32), keepdims=True)
    put_folded(out_ref, moment_ref, first_ref, count)


def side_columns(side, up, down, top, bottom, weight, noise, noise_first):
    bands = side.shape[1]
    shape = jax.ShapeDtypeStruct((bands, 256), BF16)
    return pl.pallas_call(
        corners_kernel,
        out_shape=(shape, shape, jax.ShapeDtypeStruct((2, bands // 2, 128), F32)),
        in_specs=[VMEM_SPEC] * 8,
        out_specs=(VMEM_SPEC,) * 3,
        scratch_shapes=[pltpu.VMEM((bands, bands), F32), pltpu.VMEM(noise_first.shape, F32)],
        compiler_params=params(10),
        cost_estimate=cost(2 * bands * 1024 * 128, 6 * bands * 256),
        name="side_columns",
    )(side, up, down, top, bottom, weight, noise, noise_first)


def spans_of(count):
    marks = (0, count // 6, count // 2, count)
    return list(zip(marks[:-1], marks[1:]))


def group_copy(source_ref, target_ref, sems, g):
    start = g * GROUP if isinstance(g, int) else pl.multiple_of(g * GROUP, GROUP)
    window = pl.ds(start, GROUP)
    return pltpu.make_async_copy(source_ref.at[window], target_ref.at[window], sems.at[g])


def fold(moment, columns):
    size = moment.shape[0]
    half = size // 2
    wide = moment if moment.shape[1] == 256 else jnp.concatenate(
        [moment, jnp.zeros((size, 256 - size), F32)], axis=1
    )
    row = lax.broadcasted_iota(jnp.int32, (half, 256), 0)
    lane = lax.broadcasted_iota(jnp.int32, (half, 256), 1)
    moved = pltpu.roll(wide[:half], half + 1, 1)
    out = jnp.where(lane <= half + row, wide[half:], moved)
    for place, column in enumerate(columns):
        out = jnp.where(lane == size + 2 + place, column, out)
    return out


def unfold(folded):
    half = folded.shape[0]
    size = 2 * half
    row = lax.broadcasted_iota(jnp.int32, (half, 256), 0)
    lane = lax.broadcasted_iota(jnp.int32, (half, 256), 1)
    back = pltpu.roll(folded, 256 - half - 1, 1)
    upper = jnp.where((lane >= row) & (lane < half), back, 0.0)
    lower = jnp.where(lane <= half + row, folded, 0.0)
    part = jnp.concatenate([upper, lower], axis=0)
    turned = jnp.concatenate([part, jnp.zeros((256 - size, 256), F32)], axis=0).T[:size]
    row = lax.broadcasted_iota(jnp.int32, (size, 256), 0)
    lane = lax.broadcasted_iota(jnp.int32, (size, 256), 1)
    return part + jnp.where(row == lane, 0.0, turned)


def signal_kernel(
    xt_ref, up_ref, down_ref, low_ref, high_ref, weight_ref,
    result_ref, out_ref, col_ref, moment_ref, first_ref, smooth_ref, sems,
):
    rows, bands, cols = xt_ref.shape
    groups = rows // GROUP
    moment_ref[...] = jnp.zeros_like(moment_ref)
    first_ref[...] = jnp.zeros_like(first_ref)

    def taps_of(distance):
        out = jnp.zeros(distance.shape, F32)
        for k, tap in enumerate(TAPS):
            out = jnp.where(distance == k - 2, tap, out)
        return out

    source = lax.broadcasted_iota(jnp.int32, (2 * cols, 2 * cols), 0)
    target = lax.broadcasted_iota(jnp.int32, (2 * cols, 2 * cols), 1)
    band = jnp.where(
        source // cols == target // cols, taps_of(source % cols - target % cols), 0.0
    ).astype(BF16)
    source = lax.broadcasted_iota(jnp.int32, (128, 2 * cols), 0)
    target = lax.broadcasted_iota(jnp.int32, (128, 2 * cols), 1)
    is_low = source < 16
    pixel_row = (source % 16) // 2
    position = jnp.where(is_low, source % 2 - 2, cols + source % 2)
    sides = []
    for q in range(4):
        keep = (source < 32) & (pixel_row == 2 * q + target // cols)
        sides.append(jnp.where(keep, taps_of(position - target % cols), 0.0).astype(BF16))
    lane = lax.broadcasted_iota(jnp.int32, (bands, 128), 1)

    def side_lanes(chunk, shift):
        low = low_ref[:, 128 * chunk : 128 * chunk + 128].astype(F32)
        high = high_ref[:, 128 * chunk : 128 * chunk + 128].astype(F32)
        low = pltpu.roll(low, (128 - shift) % 128, 1)
        high = pltpu.roll(high, (128 + 16 - shift) % 128, 1)
        return jnp.where(lane < 16, low, jnp.where(lane < 32, high, 0.0)).astype(BF16)

    def smooth_pair(one, two, extra, q):
        pair = jnp.concatenate([one, two], axis=1)
        out = jnp.dot(pair, band, preferred_element_type=F32)
        out += jnp.dot(extra, sides[q], preferred_element_type=F32)
        return (out[:, :cols], out[:, cols:])

    def column_pass(g):
        if g < groups:
            extra = side_lanes(g // 8, 16 * (g % 8))
            for q in range(4):
                r = g * GROUP + 2 * q
                one, two = smooth_pair(xt_ref[r], xt_ref[r + 1], extra, q)
                col_ref[r + 2] = one
                col_ref[r + 3] = two
        elif g == groups:
            extra = side_lanes(groups // 8, 16 * (groups % 8))
            one, two = smooth_pair(down_ref[0], down_ref[1], extra, 1)
            col_ref[rows + 2] = one
            col_ref[rows + 3] = two

    def row_pass(g):
        base = g * GROUP
        weights = weight_ref[base : base + GROUP, :].astype(F32)
        field = [col_ref[base + i] for i in range(GROUP + 4)]
        parts = []
        total = None
        for i in range(GROUP):
            value = (
                0.0625 * (field[i] + field[i + 4])
                + 0.25 * (field[i + 1] + field[i + 3])
                + 0.375 * field[i + 2]
            )
            smooth_ref[base + i] = value
            value = value * weights[i : i + 1, :]
            total = value if total is None else total + value
            parts.append(value.astype(BF16))
        group_copy(smooth_ref, result_ref, sems, g).start()
        first_ref[...] += total
        flat = jnp.concatenate(parts, axis=1)
        moment_ref[...] += lax.dot_general(
            flat, flat, (((1,), (1,)), ((), ())), preferred_element_type=F32
        )

    extra = side_lanes(groups // 8, 16 * (groups % 8))
    one, two = smooth_pair(up_ref[0], up_ref[1], extra, 0)
    col_ref[0] = one
    col_ref[1] = two
    column_pass(0)
    column_pass(1)
    for g in range(groups):
        column_pass(g + 2)
        row_pass(g)

    put_folded(out_ref, moment_ref, first_ref, jnp.sum(weight_ref[...].astype(F32), keepdims=True))
    for g in range(groups):
        group_copy(smooth_ref, result_ref, sems, g).wait()


def signal_moments(xt, up, down, low, high, weight):
    rows, bands, cols = xt.shape
    return pl.pallas_call(
        signal_kernel,
        out_shape=(
            pltpu.HBM((rows, bands, cols), F32),
            jax.ShapeDtypeStruct((2, bands // 2, 128), F32),
        ),
        in_specs=[VMEM_SPEC] * 6,
        out_specs=(HBM_SPEC, VMEM_SPEC),
        scratch_shapes=[
            pltpu.VMEM((rows + 4, bands, cols), F32),
            pltpu.VMEM((bands, bands), F32),
            pltpu.VMEM((bands, cols), F32),
            pltpu.VMEM((rows, bands, cols), F32),
            pltpu.SemaphoreType.DMA((rows // GROUP,)),
        ],
        compiler_params=params(32),
        cost_estimate=cost(4 * bands * bands * rows * cols, 6 * bands * rows * cols),
        name="signal_moments",
    )(in_vmem(xt), up, down, low, high, weight)


def folded_of(sums_ref):
    return jnp.concatenate([sums_ref[0], sums_ref[1]], axis=1)


def sums_of(folded):
    size = 2 * folded.shape[0]
    first = jnp.concatenate(
        [folded[:, size + 2 : size + 3], folded[:, size + 3 : size + 4]], axis=0
    )
    return (first, folded[:1, size + 4 : size + 5])


def covariance_of(folded):
    size = 2 * folded.shape[0]
    first, count = sums_of(folded)
    down = jnp.broadcast_to(first, (size, 256))
    across = jnp.concatenate([down, jnp.zeros((256 - size, 256), F32)], axis=0).T[:size]
    return (unfold(folded) - down * across / count) / (count - 1.0)


def factor_into(work_ref, size):
    width = work_ref.shape[1]
    step = PIVOTS
    sub = lax.broadcasted_iota(jnp.int32, (step, 128), 0)
    lane = lax.broadcasted_iota(jnp.int32, (step, width), 1)
    sub_wide = lax.broadcasted_iota(jnp.int32, (step, width), 0)
    for base in range(0, size, step):
        low = base + step
        panel = work_ref[base:low, :]
        cols = [
            jnp.broadcast_to(panel[:, base + j : base + j + 1], (step, 128)) for j in range(step)
        ]
        eye = jnp.where(lane - base == sub_wide, 1.0, 0.0)
        rows = jnp.where((lane >= base) & (lane < low), eye, panel)
        scale = jnp.zeros((step, 128), F32)
        for j in range(step):
            root = lax.rsqrt(jnp.broadcast_to(cols[j][j : j + 1, :], (step, 128)))
            scale = jnp.where(sub == j, root, scale)
            if j < step - 1:
                ratio = jnp.where(sub > j, cols[j] * (root * root), 0.0)
                for i in range(j + 1, step):
                    cols[i] = cols[i] - ratio * jnp.broadcast_to(
                        cols[i][j : j + 1, :], (step, 128)
                    )
                ratio_wide = jnp.concatenate([ratio, ratio], axis=1)
                rows = rows - ratio_wide * jnp.broadcast_to(rows[j : j + 1, :], (step, width))
        rows = rows * jnp.concatenate([scale, scale], axis=1)
        work_ref[base:low, :] = jnp.where(lane < low, rows, 0.0)
        if low < size:
            cut = 128 if low >= 128 else 0
            one, two, three = split_three(rows)
            left = jnp.concatenate([one, one, two, two, one, three], axis=0)
            right = jnp.concatenate([one, two, one, two, three, one], axis=0)
            update = lax.dot_general(
                left[:, cut:], right, (((0,), (0,)), ((), ())), preferred_element_type=F32
            )
            rest = work_ref[low:size, :]
            rest_lane = lax.broadcasted_iota(jnp.int32, rest.shape, 1)
            rest = jnp.where((rest_lane >= base) & (rest_lane < low), 0.0, rest)
            work_ref[low:size, :] = rest - update[low - cut : size - cut, :]


def factor_kernel(noise_ref, out_ref, work_ref):
    size = out_ref.shape[0]
    work_ref[...] = covariance_of(folded_of(noise_ref))
    factor_into(work_ref, size)
    out_ref[...] = work_ref[:, :size]


def inverse_factor(noise):
    size = 2 * noise.shape[1]
    return pl.pallas_call(
        factor_kernel,
        out_shape=jax.ShapeDtypeStruct((size, size), F32),
        in_specs=[VMEM_SPEC],
        out_specs=VMEM_SPEC,
        scratch_shapes=[pltpu.VMEM((size, 256), F32)],
        compiler_params=params(6),
        cost_estimate=cost(400 * size**3, 8 * size**2),
        name="inverse_factor",
    )(noise)


def finish_kernel(
    inverse_ref, signal_ref, weight_ref, field_ref, result_ref, cov_ref,
    smooth_ref, out_ref, in_sems, out_sems,
):
    rows, bands, cols = smooth_ref.shape
    groups, slabs = rows // GROUP, rows // 16
    for g in range(groups):
        group_copy(field_ref, smooth_ref, in_sems, g).start()
    inverse = inverse_ref[...]
    cov = covariance_of(folded_of(signal_ref))[:, :bands]
    left = jnp.dot(inverse, cov, precision=lax.Precision.HIGHEST, preferred_element_type=F32)
    cov_ref[...] = lax.dot_general(
        left, inverse, (((1,), (1,)), ((), ())),
        precision=lax.Precision.HIGHEST, preferred_element_type=F32,
    )
    inverse_cast = inverse.astype(BF16)
    first, count = sums_of(folded_of(signal_ref))
    mean = jnp.broadcast_to(first / count, (bands, cols))

    def outward(s):
        window = pl.ds(16 * s, 16)
        return pltpu.make_async_copy(out_ref.at[s], result_ref.at[:, window, :], out_sems.at[s])

    for s in range(slabs):
        base = 16 * s
        for g in (2 * s, 2 * s + 1):
            group_copy(field_ref, smooth_ref, in_sems, g).wait()
        weights = weight_ref[base : base + 16, :].astype(F32)
        parts = []
        for pair in range(8):
            pieces = []
            for i in (2 * pair, 2 * pair + 1):
                pieces.append((weights[i : i + 1, :] * (smooth_ref[base + i] - mean)).astype(BF16))
            product = jnp.dot(
                inverse_cast, jnp.concatenate(pieces, axis=1), preferred_element_type=F32
            )
            product = product.astype(BF16)
            parts += [product[None, :, :cols], product[None, :, cols:]]
        out_ref[s] = jnp.swapaxes(jnp.concatenate(parts, axis=0), 0, 1)
        outward(s).start()

    for s in range(slabs):
        outward(s).wait()


def finish(inverse, signal, weight, smooth):
    rows, bands, cols = smooth.shape
    groups, slabs = rows // GROUP, rows // 16
    return pl.pallas_call(
        finish_kernel,
        out_shape=(
            pltpu.HBM((bands, rows, cols), BF16),
            jax.ShapeDtypeStruct((bands, bands), F32),
        ),
        in_specs=[VMEM_SPEC, VMEM_SPEC, VMEM_SPEC, HBM_SPEC],
        out_specs=(HBM_SPEC, VMEM_SPEC),
        scratch_shapes=[
            pltpu.VMEM((rows, bands, cols), F32),
            pltpu.VMEM((slabs, bands, 16, cols), BF16),
            pltpu.SemaphoreType.DMA((groups,)),
            pltpu.SemaphoreType.DMA((slabs,)),
        ],
        compiler_params=params(36),
        cost_estimate=cost(2 * bands * bands * rows * cols, 6 * bands * rows * cols),
        name="finish",
    )(inverse, signal, weight, in_hbm(smooth))


def line(count):
    forward = [(i, i + 1) for i in range(count - 1)]
    return (forward, [(target, source) for source, target in forward])


def body(radiance, valid_mask):
    first, last = edge_rows(radiance)
    forward, backward = line(lax.axis_size("tile"))
    up = lax.ppermute(last, "tile", forward)
    down = lax.ppermute(first, "tile", backward)
    xt, side, noise, noise_first = rows_first(radiance, valid_mask)
    to_low, to_high, noise = side_columns(
        side, up, down, first, last, valid_mask, noise, noise_first
    )
    forward, backward = line(lax.axis_size("group"))
    low = lax.ppermute(to_high, "group", forward)
    high = lax.ppermute(to_low, "group", backward)
    smooth, signal = signal_moments(xt, up, down, low, high, valid_mask)
    noise_total, _ = total_of(noise)
    signal_total, inverse = total_of(signal, inverse_factor(noise_total))
    whitened, whitened_cov = finish(inverse, signal_total, valid_mask, smooth)
    return (whitened, whitened_cov)


def solution(mesh):
    return jax.shard_map(
        body,
        mesh=mesh,
        in_specs=(P(None, "tile", "group"), P("tile", "group")),
        out_specs=(P(None, "tile", "group"), P()),
        check_vma=False,
    )
```
